32 devices in a mesh: slab: 16 (over z, x, core), rep: 2 (over y).
Axes of the slice: x: 2, y: 2, z: 4, core: 2. Of those that a mesh axis runs over, the one named last changes fastest.
Arguments:
- dipoles: float32 [12, 256, 256], P('rep', 'slab'), parts along dimension 0, may hold values from -6 to 6
- inv_alpha: float32 [256, 256], P('slab'), may hold values from 0.5 to 2
- row_site: int32 [2, 256], P(None, 'slab'), may hold values from -1 to 63, as said below
- green: float32 [6, 128, 128, 512], P(None, None, 'slab'), may hold values from -6 to 6
Outputs:
- applied: float32 [12, 256, 256], P('rep', 'slab'), parts along dimension 0
The draws below stay inside these ranges and needn't reach their ends.
There are 2 independent parts, one for each index of `rep`. The reference program is written for one: setup_inputs(seed, part) draws one part's arguments, and reference() takes and returns one part's arrays. A program takes and returns all parts, laid end to end along the dimension named above; an argument that names none is the same for every part. Nothing has to cross between parts.
Inputs may be any that keep to these rules, and one draw needn't show every extreme that they name: `row_site`: slot r belongs to device r // 16 of slab. A live slot has y under 128 / 2 and z under 128 / 2; an empty slot has -1 in both entries. Live slots name distinct (y, z). Of one device's slots, at most 2 have z in any one block of 8 consecutive planes, and in every draw some block gets exactly 2 from every device.
All inputs are finite; a program needn't handle non-finite values.
Results may differ from the reference program's by a relative error of at most 0.00005.
Values sent between devices are 32-bit elements; how exact they have to be, the bound alone decides.
A program may use at most 128 MiB of HBM per device.

```python
import jax
import jax.numpy as jnp

NX = 256
NY = 128
NZ = 128
CAP = 2
LX = 128
ROWS = 256
N_SLAB = 16


def draw_row_site(key, part):
    devices = N_SLAB
    planes = NZ // N_SLAB
    owners = N_SLAB // 2
    candidates = NY // 2 * planes
    key_count, key_level, key_full, key_order, key_slots = jax.random.split(jax.random.fold_in(key, 11), 5)
    counts = jax.random.randint(key_count, (devices, owners), 0, CAP + 1)
    levels = jax.random.randint(key_level, (devices, 1), 2, 9)
    counts = jnp.minimum(CAP, counts * levels // 4)
    full_owner = jax.random.randint(key_full, (), 0, owners)
    counts = jnp.where(jnp.arange(owners)[None, :] == full_owner, CAP, counts)
    scores = jax.random.randint(key_order, (owners, candidates), 0, 2 ** 20) * candidates + jnp.arange(candidates)[None, :]
    ordering = jnp.argsort(scores, axis=1)
    picked = ordering[:, :devices * CAP].reshape(owners, devices, CAP).transpose(1, 0, 2)
    occupied = jnp.arange(CAP)[None, None, :] < counts[:, :, None]
    cell_y = jnp.where(occupied, picked // planes, -1).reshape(devices, owners * CAP)
    cell_z = jnp.where(occupied, jnp.arange(owners)[None, :, None] * planes + picked % planes, -1).reshape(devices, owners * CAP)
    slot_scores = jax.random.randint(key_slots, (devices, owners * CAP), 0, 2 ** 20) * (owners * CAP) + jnp.arange(owners * CAP)[None, :]
    shuffle = jnp.argsort(slot_scores, axis=1)
    cell_y = jnp.take_along_axis(cell_y, shuffle, axis=1)
    cell_z = jnp.take_along_axis(cell_z, shuffle, axis=1)
    return jnp.stack([cell_y.reshape(-1), cell_z.reshape(-1)]).astype(jnp.int32)


def shard_levels(rng, extent, cuts, smallest, largest):
    factor_of = 1.0
    for axis_at, parts in cuts:
        heights = jax.random.uniform(jax.random.fold_in(jax.random.fold_in(rng, 6), axis_at), (parts,), jnp.float32, smallest / len(cuts), largest / len(cuts))
        factor_of = factor_of * jnp.repeat(jnp.exp(heights), extent[axis_at] // parts).reshape((-1,) + (1,) * (len(extent) - 1 - axis_at))
    return factor_of


def centred(rng, extent, scale, reach, shards=(), held_as=jnp.bfloat16):
    level = shard_levels(rng, extent, shards, -0.22, 0.18) if shards else 1.0
    values = jax.random.normal(rng, extent, jnp.float32) * scale * level
    return jnp.minimum(jnp.maximum(values, -reach), reach).astype(held_as)


def setup_inputs(seed: int = 0, part: int = 0) -> dict:
    keys = jax.random.split(jax.random.key(seed), 5)
    part_splits = jax.random.split(jax.random.fold_in(keys[4], part), 5)
    dipoles = centred(part_splits[0], (6, ROWS, 2 * LX), 1.0, 6.0, ((1, 16),), jnp.float32)
    inv_alpha = jnp.clip(0.5 + 1.5 * jax.random.uniform(keys[1], (ROWS, 2 * LX), jnp.float32) ** shard_levels(keys[1], (ROWS, 2 * LX), ((0, 16),), -0.2, 0.2), 0.5, 2.0)
    row_site = draw_row_site(jax.random.fold_in(keys[4], 71), part)
    green = centred(keys[3], (6, NZ, NY, 2 * NX), 1.0, 6.0, ((2, 16),), jnp.float32)
    return dict(dipoles=dipoles, inv_alpha=inv_alpha, row_site=row_site, green=green)


def reference(dipoles, inv_alpha, row_site, green):
    occupied = row_site[0] >= 0
    cell_y = jnp.where(occupied, row_site[0], 0).astype(jnp.int32)
    cell_z = jnp.where(occupied, row_site[1], 0).astype(jnp.int32)
    row_mask = occupied.astype(jnp.float32)[None, :, None]
    source = dipoles * row_mask
    grid_values = jnp.zeros((6, NZ, NY, 2 * LX), jnp.float32).at[:, cell_z, cell_y, :].add(source)
    field = grid_values[..., :LX] + 1j * grid_values[..., LX:]
    field = jnp.pad(field, ((0, 0), (0, 0), (0, 0), (0, NX - LX)))
    spectrum = jnp.fft.fftn(field, axes=(1, 2, 3)).reshape(2, 3, NZ, NY, NX)
    kernel = green[..., :NX] + 1j * green[..., NX:]
    sym_index = ((0, 1, 2), (1, 3, 4), (2, 4, 5))
    image = jnp.stack([sum(kernel[sym_index[target][other]] * spectrum[:, other] for other in range(3)) for target in range(3)], axis=1)
    potential = jnp.fft.ifftn(image, axes=(2, 3, 4)).reshape(6, NZ, NY, NX)[..., :LX]
    picked = potential[:, cell_z, cell_y, :]
    conv_re = picked.real.astype(jnp.float32)
    conv_im = picked.imag.astype(jnp.float32)
    alpha_re = inv_alpha[:, :LX]
    alpha_im = inv_alpha[:, LX:]
    dip_re = dipoles[:, :, :LX]
    dip_im = dipoles[:, :, LX:]
    out_re = alpha_re * dip_re - alpha_im * dip_im - conv_re
    out_im = alpha_re * dip_im + alpha_im * dip_re - conv_im
    return jnp.concatenate([out_re, out_im], axis=-1) * row_mask
```

```python
import functools
import math

import jax
import jax.numpy as jnp
import numpy as np
from jax import lax
from jax.experimental import pallas as pl
from jax.experimental.pallas import tpu as pltpu
from jax.sharding import PartitionSpec as P

NX = 256
NY = 128
NZ = 128
CAP = 2


HIGH = lax.Precision.HIGHEST


def dft_table(count_in, length, count_out, direction_sign):
    index_in = jnp.arange(count_in)[:, None]
    index_out = jnp.arange(count_out)[None, :]
    phase_index = index_in * index_out % length
    angles = phase_index.astype(jnp.float32) * (2.0 * math.pi / length)
    cosine = jnp.cos(angles)
    sine_part = jnp.sin(angles) * direction_sign
    factor = 1.0 if direction_sign < 0 else 1.0 / length
    upper_rows = jnp.concatenate([cosine, sine_part], axis=1)
    lower_rows = jnp.concatenate([-sine_part, cosine], axis=1)
    return jnp.concatenate([upper_rows, lower_rows], axis=0) * factor


def middle_transform(values, count_in, length, count_out, direction_sign, pattern):
    index_out = jnp.arange(count_out)[:, None]
    index_in = jnp.arange(count_in)[None, :]
    angles = (index_out * index_in % length).astype(jnp.float32) * (2.0 * math.pi / length)
    factor = 1.0 if direction_sign < 0 else 1.0 / length
    cosine = jnp.cos(angles) * factor
    sine_part = jnp.sin(angles) * (direction_sign * factor)
    mixed_cos = jnp.einsum(pattern, cosine, values, precision=HIGH)
    mixed_sin = jnp.einsum(pattern, sine_part, values, precision=HIGH)
    half_width = values.shape[-1] // 2
    real_part = mixed_cos[..., :half_width] - mixed_sin[..., half_width:]
    imag_part = mixed_cos[..., half_width:] + mixed_sin[..., :half_width]
    return jnp.concatenate([real_part, imag_part], axis=-1)


def apply_kernel(spectrum, green):
    half_width = spectrum.shape[-1] // 2
    sym_index = ((0, 1, 2), (1, 3, 4), (2, 4, 5))
    results = []
    for vector in range(2):
        for target in range(3):
            total_re = jnp.zeros(spectrum.shape[1:-1] + (half_width,), jnp.float32)
            total_im = jnp.zeros(spectrum.shape[1:-1] + (half_width,), jnp.float32)
            for other in range(3):
                kernel = green[sym_index[target][other]]
                source = spectrum[vector * 3 + other]
                kern_re, kern_im = (kernel[..., :half_width], kernel[..., half_width:])
                src_re, src_im = (source[..., :half_width], source[..., half_width:])
                total_re = total_re + kern_re * src_re - kern_im * src_im
                total_im = total_im + kern_re * src_im + kern_im * src_re
            results.append(jnp.concatenate([total_re, total_im], axis=-1))
    return jnp.stack(results, axis=0)


def planes_body(dipoles, inv_alpha, row_site, green):
    devices = lax.axis_size("slab")
    row_len = dipoles.shape[2] // 2
    planes = NZ // 2 // devices
    half_y = NY // 2
    half_z = NZ // 2
    occupied = row_site[0] >= 0
    dest_dev = jnp.where(occupied, row_site[1] // planes, -1)
    local_pos = row_site[1] % planes * half_y + row_site[0]
    slots_all = devices * CAP
    owner_hot = (dest_dev[:, None] == jnp.arange(devices)[None, :]).astype(jnp.int32)
    earlier = jnp.cumsum(owner_hot, axis=0) - owner_hot
    slot_index = jnp.sum(earlier * owner_hot, axis=1)
    target = jnp.where(occupied, dest_dev * CAP + slot_index, -1)
    packer = target[None, :] == jnp.arange(slots_all)[:, None]
    pack_float = packer.astype(jnp.float32)
    send_rows = jnp.einsum("qr,vrx->vqx", pack_float, dipoles, precision=HIGH)
    send_pos = jnp.sum(jnp.where(packer, local_pos[None, :] + 1, 0), axis=1) - 1
    send_pos = send_pos.astype(jnp.float32)[None, :]
    recv_rows, recv_pos = (
        lax.all_to_all(send_rows, "slab", split_axis=1, concat_axis=1, tiled=True),
        lax.all_to_all(send_pos, "slab", split_axis=1, concat_axis=1, tiled=True),
    )
    table_x = dft_table(row_len, NX, NX, -1)
    spectral_rows = jnp.einsum("vqx,xk->vqk", recv_rows, table_x, precision=HIGH)
    plane_cells = planes * half_y
    placer = (recv_pos[0].astype(jnp.int32)[None, :] == jnp.arange(plane_cells)[:, None]).astype(
        jnp.float32
    )
    plane_grid = jnp.einsum("cq,vqk->vck", placer, spectral_rows, precision=HIGH)
    plane_grid = plane_grid.reshape(6, planes, half_y, 2 * NX)
    y_spectrum = middle_transform(plane_grid, half_y, NY, NY, -1, "ky,vzyx->vzkx")
    z_spectrum = middle_transform(
        lax.all_to_all(y_spectrum, "slab", split_axis=2, concat_axis=1, tiled=True),
        half_z,
        NZ,
        NZ,
        -1,
        "kz,vzyx->vkyx",
    )
    image = apply_kernel(z_spectrum, green)
    z_back = middle_transform(image, NZ, NZ, half_z, 1, "kz,vzyx->vkyx")
    fields = middle_transform(
        lax.all_to_all(z_back, "slab", split_axis=1, concat_axis=2, tiled=True),
        NY,
        NY,
        half_y,
        1,
        "ky,vzyx->vzkx",
    )
    flat_fields = fields.reshape(6, plane_cells, 2 * NX)
    picked = jnp.einsum("cq,vck->vqk", placer, flat_fields, precision=HIGH)
    table_back = dft_table(NX, NX, row_len, 1)
    back_rows = jnp.einsum("vqk,kx->vqx", picked, table_back, precision=HIGH)
    returned = jnp.einsum(
        "qr,vqx->vrx",
        pack_float,
        lax.all_to_all(back_rows, "slab", split_axis=1, concat_axis=1, tiled=True),
        precision=HIGH,
    )
    row_mask = occupied.astype(jnp.float32)[None, :, None]
    alpha_re = inv_alpha[:, :row_len]
    alpha_im = inv_alpha[:, row_len:]
    dip_re = dipoles[:, :, :row_len]
    dip_im = dipoles[:, :, row_len:]
    out_re = alpha_re * dip_re - alpha_im * dip_im - returned[:, :, :row_len]
    out_im = alpha_re * dip_im + alpha_im * dip_re - returned[:, :, row_len:]
    return jnp.concatenate([out_re, out_im], axis=-1) * row_mask


BF = jnp.bfloat16
F32 = jnp.float32
SYM = ((0, 1, 2), (1, 3, 4), (2, 4, 5))


def split(values):
    high = values.astype(BF)
    return high, (values - high.astype(F32)).astype(BF)


def left3(values):
    high, low = split(values)
    return jnp.concatenate([high, high, low], axis=1)


def right3(values):
    high, low = split(values)
    return jnp.concatenate([high, low, high], axis=0)


def mm(left, right):
    return jnp.dot(left, right, preferred_element_type=F32)


def trig(rows, cols, length):
    angles = 2.0 * np.pi * (np.arange(rows)[:, None] * np.arange(cols)[None, :] % length) / length
    return np.cos(angles), np.sin(angles)


def stack3(table):
    return right3(jnp.asarray(table.astype(np.float32)))


def spectral_kernel(
    rows_ref, site_ref, green_ref, ty_ref, tz_ref, tx_ref, tb_ref, out_ref,
    xs, ez, ey, spec, img, acc,
):
    step = pl.program_id(0)
    steps = pl.num_programs(0)
    n_dev, comps, per_dev, width = rows_ref.shape
    n_rows = n_dev * per_dev
    kz_block, ky_count = green_ref.shape[1], green_ref.shape[2]
    nx = green_ref.shape[3] // 2
    cells = kz_block * ky_count

    @pl.when(step == 0)
    def _():
        acc[...] = jnp.zeros_like(acc)
        for axis, (table, dest) in enumerate(((ty_ref, ey), (tz_ref, ez))):
            sites = site_ref[axis : axis + 1, :]
            half = table.shape[2]
            hot = (lax.broadcasted_iota(jnp.int32, (half, n_rows), 0) == sites).astype(F32)
            for part in range(2):
                dest[part] = jnp.dot(table[part], hot, precision=HIGH, preferred_element_type=F32)
        for c in range(comps):
            rows = rows_ref[:, c].reshape(n_rows, width)
            x = mm(left3(rows), tx_ref[...])
            x_re, x_im = x[:, :nx], x[:, nx:]
            xs[0, c] = right3(x_re)
            xs[1, c] = right3(x_im)
            xs[2, c] = right3(x_re + x_im)

    zc = ez[0, pl.ds(step * kz_block, kz_block), :][:, None, :]
    zs = ez[1, pl.ds(step * kz_block, kz_block), :][:, None, :]
    yc = ey[0][None]
    ys = ey[1][None]
    a = (zc * yc - zs * ys).reshape(cells, n_rows)
    b = -(zc * ys + zs * yc).reshape(cells, n_rows)
    fa, fb, fab = left3(a), left3(b), left3(a + b)
    for c in range(comps):
        p1 = mm(fa, xs[0, c])
        p2 = mm(fb, xs[1, c])
        p3 = mm(fab, xs[2, c])
        spec[c, 0] = p1 - p2
        spec[c, 1] = p3 - p1 - p2

    a_t = a.T
    b_t = -b.T
    ga, gb, gab = left3(a_t), left3(b_t), left3(a_t + b_t)

    kz_chunk = max(1, 16 // ky_count)
    chunk = kz_chunk * ky_count

    def apply_chunk(j, carry):
        row = pl.multiple_of(j * chunk, chunk)
        for lane in range(0, nx, 128):
            g = [
                [
                    green_ref[m, pl.ds(j * kz_chunk, kz_chunk), :, pl.ds(part * nx + lane, 128)].reshape(chunk, 128)
                    for part in range(2)
                ]
                for m in range(6)
            ]
            for v in range(comps // 3):
                s = [[spec[3 * v + o, part, pl.ds(row, chunk), pl.ds(lane, 128)] for part in range(2)] for o in range(3)]
                for t in range(3):
                    re = im = None
                    for o in range(3):
                        k_re, k_im = g[SYM[t][o]]
                        s_re, s_im = s[o]
                        d_re = k_re * s_re - k_im * s_im
                        d_im = k_re * s_im + k_im * s_re
                        re = d_re if re is None else re + d_re
                        im = d_im if im is None else im + d_im
                    for kind, value in enumerate((re, im, re + im)):
                        high, low = split(value)
                        img[kind, 3 * v + t, 0, pl.ds(row, chunk), pl.ds(lane, 128)] = high
                        img[kind, 3 * v + t, 1, pl.ds(row, chunk), pl.ds(lane, 128)] = low
        return carry

    lax.fori_loop(0, kz_block // kz_chunk, apply_chunk, 0)

    for c in range(comps):
        for kind, left in enumerate((ga, gb, gab)):
            high = img[kind, c, 0]
            low = img[kind, c, 1]
            acc[kind, c] += mm(left, jnp.concatenate([high, low, high], axis=0))

    @pl.when(step == steps - 1)
    def _():
        for c in range(comps):
            p1, p2, p3 = acc[0, c], acc[1, c], acc[2, c]
            both = jnp.concatenate([p1 - p2, p3 - p1 - p2], axis=1)
            out_ref[:, c] = mm(left3(both), tb_ref[...]).reshape(n_dev, per_dev, width)


def spectral(rows, sites, green, nx, ny, nz):
    n_dev, comps, per_dev, width = rows.shape
    n_rows = n_dev * per_dev
    ky_count = green.shape[2]
    row_len = width // 2
    kz_block = 256 // ky_count
    cos_x, sin_x = trig(row_len, nx, nx)
    forward_x = np.block([[cos_x, -sin_x], [sin_x, cos_x]])
    back_x = np.block([[cos_x.T, sin_x.T], [-sin_x.T, cos_x.T]]) / float(nx * ny * nz)
    table_y = jnp.asarray(np.stack(trig(ny, ny // 2, ny)).astype(np.float32))
    table_y = lax.dynamic_slice_in_dim(table_y, lax.axis_index("slab") * ky_count, ky_count, 1)
    table_z = jnp.asarray(np.stack(trig(nz, nz // 2, nz)).astype(np.float32))
    whole = lambda: pl.BlockSpec(memory_space=pltpu.VMEM)
    return pl.pallas_call(
        spectral_kernel,
        grid=(nz // kz_block,),
        out_shape=jax.ShapeDtypeStruct(rows.shape, F32),
        in_specs=[
            whole(),
            whole(),
            pl.BlockSpec((6, kz_block, ky_count, 2 * nx), lambda i: (0, i, 0, 0)),
            whole(),
            whole(),
            whole(),
            whole(),
        ],
        out_specs=pl.BlockSpec(memory_space=pltpu.VMEM),
        scratch_shapes=[
            pltpu.VMEM((3, comps, 3 * n_rows, nx), BF),
            pltpu.VMEM((2, nz, n_rows), F32),
            pltpu.VMEM((2, ky_count, n_rows), F32),
            pltpu.VMEM((comps, 2, kz_block * ky_count, nx), F32),
            pltpu.VMEM((3, comps, 2, kz_block * ky_count, nx), BF),
            pltpu.VMEM((3, comps, n_rows, nx), F32),
        ],
        compiler_params=pltpu.CompilerParams(vmem_limit_bytes=60000 * 1024),
    )(rows, sites, green, table_y, table_z, stack3(forward_x), stack3(back_x))


def rows_body(dipoles, inv_alpha, row_site, green):
    row_len = dipoles.shape[2] // 2
    nz = green.shape[1]
    nx = green.shape[3] // 2
    ny = green.shape[2] * lax.axis_size("slab")
    rows = lax.all_gather(dipoles, "slab", axis=0)
    sites = lax.all_gather(row_site.astype(F32), "slab", axis=1, tiled=True).astype(jnp.int32)
    partial = spectral(rows, sites, green, nx, ny, nz)
    returned = lax.psum_scatter(partial, "slab", scatter_dimension=0, tiled=False)
    row_mask = (row_site[0] >= 0)[None, :, None]
    alpha_re = inv_alpha[:, :row_len]
    alpha_im = inv_alpha[:, row_len:]
    dip_re = dipoles[:, :, :row_len]
    dip_im = dipoles[:, :, row_len:]
    out_re = alpha_re * dip_re - alpha_im * dip_im - returned[:, :, :row_len]
    out_im = alpha_re * dip_im + alpha_im * dip_re - returned[:, :, row_len:]
    return jnp.where(row_mask, jnp.concatenate([out_re, out_im], axis=-1), 0.0)


def body(dipoles, inv_alpha, row_site, green):
    n_rows = dipoles.shape[1] * lax.axis_size("slab")
    spectra_bytes = 4 * dipoles.shape[0] * n_rows * green.shape[3]
    if spectra_bytes <= 4 * 2**20 and green.shape[2] % 8 == 0:
        return rows_body(dipoles, inv_alpha, row_site, green)
    return planes_body(dipoles, inv_alpha, row_site, green)


def solution(mesh):
    return jax.shard_map(
        body,
        mesh=mesh,
        in_specs=(
            P("rep", "slab", None),
            P("slab", None),
            P(None, "slab"),
            P(None, None, "slab", None),
        ),
        out_specs=P("rep", "slab", None),
        check_vma=False,
    )
```

```python
import functools
import math

import jax
import jax.numpy as jnp
import numpy as np
from jax import lax
from jax.experimental import pallas as pl
from jax.experimental.pallas import tpu as pltpu
from jax.sharding import PartitionSpec as P

NX = 256
NY = 128
NZ = 128
CAP = 2


HIGH = lax.Precision.HIGHEST


def dft_table(count_in, length, count_out, direction_sign):
    index_in = jnp.arange(count_in)[:, None]
    index_out = jnp.arange(count_out)[None, :]
    phase_index = index_in * index_out % length
    angles = phase_index.astype(jnp.float32) * (2.0 * math.pi / length)
    cosine = jnp.cos(angles)
    sine_part = jnp.sin(angles) * direction_sign
    factor = 1.0 if direction_sign < 0 else 1.0 / length
    upper_rows = jnp.concatenate([cosine, sine_part], axis=1)
    lower_rows = jnp.concatenate([-sine_part, cosine], axis=1)
    return jnp.concatenate([upper_rows, lower_rows], axis=0) * factor


def middle_transform(values, count_in, length, count_out, direction_sign, pattern):
    index_out = jnp.arange(count_out)[:, None]
    index_in = jnp.arange(count_in)[None, :]
    angles = (index_out * index_in % length).astype(jnp.float32) * (2.0 * math.pi / length)
    factor = 1.0 if direction_sign < 0 else 1.0 / length
    cosine = jnp.cos(angles) * factor
    sine_part = jnp.sin(angles) * (direction_sign * factor)
    mixed_cos = jnp.einsum(pattern, cosine, values, precision=HIGH)
    mixed_sin = jnp.einsum(pattern, sine_part, values, precision=HIGH)
    half_width = values.shape[-1] // 2
    real_part = mixed_cos[..., :half_width] - mixed_sin[..., half_width:]
    imag_part = mixed_cos[..., half_width:] + mixed_sin[..., :half_width]
    return jnp.concatenate([real_part, imag_part], axis=-1)


def apply_kernel(spectrum, green):
    half_width = spectrum.shape[-1] // 2
    sym_index = ((0, 1, 2), (1, 3, 4), (2, 4, 5))
    results = []
    for vector in range(2):
        for target in range(3):
            total_re = jnp.zeros(spectrum.shape[1:-1] + (half_width,), jnp.float32)
            total_im = jnp.zeros(spectrum.shape[1:-1] + (half_width,), jnp.float32)
            for other in range(3):
                kernel = green[sym_index[target][other]]
                source = spectrum[vector * 3 + other]
                kern_re, kern_im = (kernel[..., :half_width], kernel[..., half_width:])
                src_re, src_im = (source[..., :half_width], source[..., half_width:])
                total_re = total_re + kern_re * src_re - kern_im * src_im
                total_im = total_im + kern_re * src_im + kern_im * src_re
            results.append(jnp.concatenate([total_re, total_im], axis=-1))
    return jnp.stack(results, axis=0)


def planes_body(dipoles, inv_alpha, row_site, green):
    devices = lax.axis_size("slab")
    row_len = dipoles.shape[2] // 2
    planes = NZ // 2 // devices
    half_y = NY // 2
    half_z = NZ // 2
    occupied = row_site[0] >= 0
    dest_dev = jnp.where(occupied, row_site[1] // planes, -1)
    local_pos = row_site[1] % planes * half_y + row_site[0]
    slots_all = devices * CAP
    owner_hot = (dest_dev[:, None] == jnp.arange(devices)[None, :]).astype(jnp.int32)
    earlier = jnp.cumsum(owner_hot, axis=0) - owner_hot
    slot_index = jnp.sum(earlier * owner_hot, axis=1)
    target = jnp.where(occupied, dest_dev * CAP + slot_index, -1)
    packer = target[None, :] == jnp.arange(slots_all)[:, None]
    pack_float = packer.astype(jnp.float32)
    send_rows = jnp.einsum("qr,vrx->vqx", pack_float, dipoles, precision=HIGH)
    send_pos = jnp.sum(jnp.where(packer, local_pos[None, :] + 1, 0), axis=1) - 1
    send_pos = send_pos.astype(jnp.float32)[None, :]
    recv_rows, recv_pos = (
        lax.all_to_all(send_rows, "slab", split_axis=1, concat_axis=1, tiled=True),
        lax.all_to_all(send_pos, "slab", split_axis=1, concat_axis=1, tiled=True),
    )
    table_x = dft_table(row_len, NX, NX, -1)
    spectral_rows = jnp.einsum("vqx,xk->vqk", recv_rows, table_x, precision=HIGH)
    plane_cells = planes * half_y
    placer = (recv_pos[0].astype(jnp.int32)[None, :] == jnp.arange(plane_cells)[:, None]).astype(
        jnp.float32
    )
    plane_grid = jnp.einsum("cq,vqk->vck", placer, spectral_rows, precision=HIGH)
    plane_grid = plane_grid.reshape(6, planes, half_y, 2 * NX)
    y_spectrum = middle_transform(plane_grid, half_y, NY, NY, -1, "ky,vzyx->vzkx")
    z_spectrum = middle_transform(
        lax.all_to_all(y_spectrum, "slab", split_axis=2, concat_axis=1, tiled=True),
        half_z,
        NZ,
        NZ,
        -1,
        "kz,vzyx->vkyx",
    )
    image = apply_kernel(z_spectrum, green)
    z_back = middle_transform(image, NZ, NZ, half_z, 1, "kz,vzyx->vkyx")
    fields = middle_transform(
        lax.all_to_all(z_back, "slab", split_axis=1, concat_axis=2, tiled=True),
        NY,
        NY,
        half_y,
        1,
        "ky,vzyx->vzkx",
    )
    flat_fields = fields.reshape(6, plane_cells, 2 * NX)
    picked = jnp.einsum("cq,vck->vqk", placer, flat_fields, precision=HIGH)
    table_back = dft_table(NX, NX, row_len, 1)
    back_rows = jnp.einsum("vqk,kx->vqx", picked, table_back, precision=HIGH)
    returned = jnp.einsum(
        "qr,vqx->vrx",
        pack_float,
        lax.all_to_all(back_rows, "slab", split_axis=1, concat_axis=1, tiled=True),
        precision=HIGH,
    )
    row_mask = occupied.astype(jnp.float32)[None, :, None]
    alpha_re = inv_alpha[:, :row_len]
    alpha_im = inv_alpha[:, row_len:]
    dip_re = dipoles[:, :, :row_len]
    dip_im = dipoles[:, :, row_len:]
    out_re = alpha_re * dip_re - alpha_im * dip_im - returned[:, :, :row_len]
    out_im = alpha_re * dip_im + alpha_im * dip_re - returned[:, :, row_len:]
    return jnp.concatenate([out_re, out_im], axis=-1) * row_mask


BF = jnp.bfloat16
F32 = jnp.float32
SYM = ((0, 1, 2), (1, 3, 4), (2, 4, 5))


def split(values):
    high = values.astype(BF)
    return high, (values - high.astype(F32)).astype(BF)


def left3(values):
    high, low = split(values)
    return jnp.concatenate([high, high, low], axis=1)


def right3(values):
    high, low = split(values)
    return jnp.concatenate([high, low, high], axis=0)


def mm(left, right):
    return jnp.dot(left, right, preferred_element_type=F32)


def trig(rows, cols, length):
    angles = 2.0 * np.pi * (np.arange(rows)[:, None] * np.arange(cols)[None, :] % length) / length
    return np.cos(angles), np.sin(angles)


def stack3(table):
    return right3(jnp.asarray(table.astype(np.float32)))


def spectral_kernel(
    rows_ref, green_ref, ty_ref, tz_ref, tx_ref, tb_ref, out_ref,
    xs, ez, ey, spec, img, acc,
):
    step = pl.program_id(0)
    steps = pl.num_programs(0)
    n_dev, comps, per_dev, width = out_ref.shape
    n_rows = n_dev * per_dev
    kz_block, ky_count = green_ref.shape[1], green_ref.shape[2]
    nx = green_ref.shape[3] // 2
    cells = kz_block * ky_count

    @pl.when(step == 0)
    def _():
        acc[...] = jnp.zeros_like(acc)
        sites = rows_ref[:, comps].reshape(n_rows, width)
        for axis, (table, dest) in enumerate(((ty_ref, ey), (tz_ref, ez))):
            half = table.shape[2]
            column = sites[:, axis : axis + 1].astype(jnp.int32)
            hot = (lax.broadcasted_iota(jnp.int32, (n_rows, half), 1) == column).astype(F32)
            for part in range(2):
                dest[part] = lax.dot_general(
                    table[part], hot, (((1,), (1,)), ((), ())), precision=HIGH, preferred_element_type=F32
                )
        for c in range(comps):
            rows = rows_ref[:, c].reshape(n_rows, width)
            x = mm(left3(rows), tx_ref[...])
            x_re, x_im = x[:, :nx], x[:, nx:]
            xs[0, c] = right3(x_re)
            xs[1, c] = right3(x_im)
            xs[2, c] = right3(x_re + x_im)

    zc = ez[0, pl.ds(step * kz_block, kz_block), :][:, None, :]
    zs = ez[1, pl.ds(step * kz_block, kz_block), :][:, None, :]
    yc = ey[0][None]
    ys = ey[1][None]
    a = (zc * yc - zs * ys).reshape(cells, n_rows)
    b = -(zc * ys + zs * yc).reshape(cells, n_rows)
    fa, fb, fab = left3(a), left3(b), left3(a + b)
    for c in range(comps):
        p1 = mm(fa, xs[0, c])
        p2 = mm(fb, xs[1, c])
        p3 = mm(fab, xs[2, c])
        spec[c, 0] = p1 - p2
        spec[c, 1] = p3 - p1 - p2

    a_t = a.T
    b_t = -b.T
    ga, gb, gab = left3(a_t), left3(b_t), left3(a_t + b_t)

    kz_chunk = max(1, 16 // ky_count)
    chunk = kz_chunk * ky_count

    def apply_chunk(j, carry):
        row = pl.multiple_of(j * chunk, chunk)
        for lane in range(0, nx, 128):
            g = [
                [
                    green_ref[m, pl.ds(j * kz_chunk, kz_chunk), :, pl.ds(part * nx + lane, 128)].reshape(chunk, 128)
                    for part in range(2)
                ]
                for m in range(6)
            ]
            for v in range(comps // 3):
                s = [[spec[3 * v + o, part, pl.ds(row, chunk), pl.ds(lane, 128)] for part in range(2)] for o in range(3)]
                for t in range(3):
                    re = im = None
                    for o in range(3):
                        k_re, k_im = g[SYM[t][o]]
                        s_re, s_im = s[o]
                        d_re = k_re * s_re - k_im * s_im
                        d_im = k_re * s_im + k_im * s_re
                        re = d_re if re is None else re + d_re
                        im = d_im if im is None else im + d_im
                    for kind, value in enumerate((re, im, re + im)):
                        high, low = split(value)
                        img[kind, 3 * v + t, 0, pl.ds(row, chunk), pl.ds(lane, 128)] = high
                        img[kind, 3 * v + t, 1, pl.ds(row, chunk), pl.ds(lane, 128)] = low
        return carry

    lax.fori_loop(0, kz_block // kz_chunk, apply_chunk, 0)

    for c in range(comps):
        for kind, left in enumerate((ga, gb, gab)):
            high = img[kind, c, 0]
            low = img[kind, c, 1]
            acc[kind, c] += mm(left, jnp.concatenate([high, low, high], axis=0))

    @pl.when(step == steps - 1)
    def _():
        for c in range(comps):
            p1, p2, p3 = acc[0, c], acc[1, c], acc[2, c]
            both = jnp.concatenate([p1 - p2, p3 - p1 - p2], axis=1)
            out_ref[:, c] = mm(left3(both), tb_ref[...]).reshape(n_dev, per_dev, width)


def spectral(rows, green, nx, ny, nz):
    n_dev, planes, per_dev, width = rows.shape
    comps = planes - 1
    n_rows = n_dev * per_dev
    ky_count = green.shape[2]
    row_len = width // 2
    kz_block = 256 // ky_count
    cos_x, sin_x = trig(row_len, nx, nx)
    forward_x = np.block([[cos_x, -sin_x], [sin_x, cos_x]])
    back_x = np.block([[cos_x.T, sin_x.T], [-sin_x.T, cos_x.T]]) / float(nx * ny * nz)
    table_y = jnp.asarray(np.stack(trig(ny, ny // 2, ny)).astype(np.float32))
    table_y = lax.dynamic_slice_in_dim(table_y, lax.axis_index("slab") * ky_count, ky_count, 1)
    table_z = jnp.asarray(np.stack(trig(nz, nz // 2, nz)).astype(np.float32))
    whole = lambda: pl.BlockSpec(memory_space=pltpu.VMEM)
    return pl.pallas_call(
        spectral_kernel,
        grid=(nz // kz_block,),
        out_shape=jax.ShapeDtypeStruct((n_dev, comps, per_dev, width), F32),
        in_specs=[
            whole(),
            pl.BlockSpec((6, kz_block, ky_count, 2 * nx), lambda i: (0, i, 0, 0)),
            whole(),
            whole(),
            whole(),
            whole(),
        ],
        out_specs=pl.BlockSpec(memory_space=pltpu.VMEM),
        scratch_shapes=[
            pltpu.VMEM((3, comps, 3 * n_rows, nx), BF),
            pltpu.VMEM((2, nz, n_rows), F32),
            pltpu.VMEM((2, ky_count, n_rows), F32),
            pltpu.VMEM((comps, 2, kz_block * ky_count, nx), F32),
            pltpu.VMEM((3, comps, 2, kz_block * ky_count, nx), BF),
            pltpu.VMEM((3, comps, n_rows, nx), F32),
        ],
        compiler_params=pltpu.CompilerParams(vmem_limit_bytes=60000 * 1024),
    )(rows, green, table_y, table_z, stack3(forward_x), stack3(back_x))


def place(n_dev):
    me = lax.axis_index("slab")
    return me, me // 4, (me // 2) % 2, me % 2, n_dev // 4


def slot_of(z, x, core):
    return (z * 2 + x) * 2 + core


def greet(z, x, core, depth):
    barrier = pltpu.get_barrier_semaphore()
    peers = [slot_of(z, 1 - x, core), slot_of(z, x, 1 - core)]
    peers += [slot_of((z + d) % depth, x, core) for d in range(1, depth)]
    for peer in peers:
        pl.semaphore_signal(barrier, inc=1, device_id={"slab": peer}, device_id_type=pl.DeviceIdType.MESH)
    pl.semaphore_wait(barrier, len(peers))


def send(src, dst, send_sem, recv_sem, peer):
    copy = pltpu.make_async_remote_copy(
        src_ref=src,
        dst_ref=dst,
        send_sem=send_sem,
        recv_sem=recv_sem,
        device_id={"slab": peer},
        device_id_type=pl.DeviceIdType.MESH,
    )
    copy.start()
    return copy


def site_columns(site_ref):
    per_dev = site_ref.shape[1]
    row = lax.broadcasted_iota(jnp.int32, (per_dev, per_dev), 0)
    col = lax.broadcasted_iota(jnp.int32, (per_dev, per_dev), 1)
    return [
        jnp.sum(jnp.where(row == col, site_ref[axis : axis + 1, :].astype(F32), 0.0), axis=1, keepdims=True)
        for axis in range(2)
    ]


def gather_kernel(dip_ref, site_ref, all_ref, send_z, recv_z, send_x, recv_x, send_c, recv_c):
    n_dev = all_ref.shape[0]
    comps, per_dev, width = dip_ref.shape
    me, z, x, core, depth = place(n_dev)
    all_ref[me, pl.ds(0, comps)] = dip_ref[...]
    y_col, z_col = site_columns(site_ref)
    lane = lax.broadcasted_iota(jnp.int32, (per_dev, width), 1)
    all_ref[me, comps] = jnp.where(lane == 0, y_col, z_col)
    greet(z, x, core, depth)
    x_peer, c_peer = slot_of(z, 1 - x, core), slot_of(z, x, 1 - core)
    order = sorted(range(1, depth), key=lambda d: min(d, depth - d))
    zs, xs, cs = {}, {}, {}
    for d in order:
        zs[d] = send(all_ref.at[me], all_ref.at[me], send_z.at[d], recv_z.at[d], slot_of((z + d) % depth, x, core))

    def pass_on(d):
        slot = all_ref.at[slot_of((z - d + depth) % depth, x, core)]
        xs[d] = send(slot, slot, send_x.at[d], recv_x.at[d], x_peer)
        cs[d, 0] = send(slot, slot, send_c.at[d], recv_c.at[d], c_peer)

    def cross(d):
        xs[d].wait_recv()
        slot = all_ref.at[slot_of((z - d + depth) % depth, 1 - x, core)]
        cs[d, 1] = send(slot, slot, send_c.at[depth + d], recv_c.at[depth + d], c_peer)

    pass_on(0)
    before = 0
    for d in order:
        zs[d].wait_recv()
        pass_on(d)
        cross(before)
        before = d
    cross(before)
    for copy in cs.values():
        copy.wait_recv()
    for copy in [*zs.values(), *xs.values(), *cs.values()]:
        copy.wait_send()


def gather_rows(dipoles, row_site):
    n_dev = lax.axis_size("slab")
    depth = n_dev // 4
    comps, per_dev, width = dipoles.shape
    dma = pltpu.SemaphoreType.DMA
    return pl.pallas_call(
        gather_kernel,
        out_shape=jax.ShapeDtypeStruct((n_dev, comps + 1, per_dev, width), F32),
        in_specs=[pl.BlockSpec(memory_space=pltpu.VMEM)] * 2,
        out_specs=pl.BlockSpec(memory_space=pltpu.VMEM),
        scratch_shapes=[dma((depth,)), dma((depth,)), dma((depth,)), dma((depth,)), dma((2 * depth,)), dma((2 * depth,))],
        compiler_params=pltpu.CompilerParams(collective_id=0, has_side_effects=True),
    )(dipoles, row_site)


def reduce_kernel(
    part_ref, dip_ref, alpha_ref, site_ref, out_ref,
    got_c, got_x, got_z, sum_x, sum_z, send_c, recv_c, send_x, recv_x, send_z, recv_z,
):
    n_dev, comps, per_dev, width = part_ref.shape
    row_len = width // 2
    me, z, x, core, depth = place(n_dev)
    greet(z, x, core, depth)
    x_peer, c_peer = slot_of(z, 1 - x, core), slot_of(z, x, 1 - core)
    order = sorted(range(1, depth), key=lambda d: -min(d, depth - d)) + [0]
    xs, cs, zs = {}, {}, {}
    for half, x_to in ((0, 1 - x), (1, x)):
        for d in order:
            slot = slot_of((z + d) % depth, x_to, 1 - core)
            k = half * depth + d
            cs[half, d] = send(part_ref.at[slot], got_c.at[k], send_c.at[k], recv_c.at[k], c_peer)
    for d in order:
        cs[0, d].wait_recv()
        sum_x[d] = part_ref[slot_of((z + d) % depth, 1 - x, core)] + got_c[d]
        xs[d] = send(sum_x.at[d], got_x.at[d], send_x.at[d], recv_x.at[d], x_peer)
    for d in order:
        cs[1, d].wait_recv()
        xs[d].wait_recv()
        sum_z[d] = part_ref[slot_of((z + d) % depth, x, core)] + got_c[depth + d] + got_x[d]
        if d:
            zs[d] = send(sum_z.at[d], got_z.at[d], send_z.at[d], recv_z.at[d], slot_of((z + d) % depth, x, core))
    a_re, a_im = alpha_ref[:, :row_len], alpha_ref[:, row_len:]
    y_col, _ = site_columns(site_ref)
    live = y_col >= 0.0
    for copy in zs.values():
        copy.wait_recv()
    for c in range(comps):
        total = sum_z[0, c]
        for d in range(1, depth):
            total = total + got_z[d, c]
        d_re, d_im = dip_ref[c, :, :row_len], dip_ref[c, :, row_len:]
        o_re = a_re * d_re - a_im * d_im - total[:, :row_len]
        o_im = a_re * d_im + a_im * d_re - total[:, row_len:]
        out_ref[c] = jnp.where(live, jnp.concatenate([o_re, o_im], axis=1), 0.0)
    for copy in [*zs.values(), *xs.values(), *cs.values()]:
        copy.wait_send()


def reduce_rows(partial, dipoles, inv_alpha, row_site):
    n_dev, *block = partial.shape
    depth = n_dev // 4
    dma = pltpu.SemaphoreType.DMA
    hold = lambda count: pltpu.VMEM((count, *block), F32)
    return pl.pallas_call(
        reduce_kernel,
        out_shape=jax.ShapeDtypeStruct(dipoles.shape, F32),
        in_specs=[pl.BlockSpec(memory_space=pltpu.VMEM)] * 4,
        out_specs=pl.BlockSpec(memory_space=pltpu.VMEM),
        scratch_shapes=[
            hold(2 * depth), hold(depth), hold(depth), hold(depth), hold(depth),
            dma((2 * depth,)), dma((2 * depth,)), dma((depth,)), dma((depth,)), dma((depth,)), dma((depth,)),
        ],
        compiler_params=pltpu.CompilerParams(collective_id=1, has_side_effects=True),
    )(partial, dipoles, inv_alpha, row_site)


def rows_body(dipoles, inv_alpha, row_site, green):
    nz = green.shape[1]
    nx = green.shape[3] // 2
    ny = green.shape[2] * lax.axis_size("slab")
    rows = gather_rows(dipoles, row_site)
    partial = spectral(rows, green, nx, ny, nz)
    return reduce_rows(partial, dipoles, inv_alpha, row_site)


def body(dipoles, inv_alpha, row_site, green):
    n_rows = dipoles.shape[1] * lax.axis_size("slab")
    spectra_bytes = 4 * dipoles.shape[0] * n_rows * green.shape[3]
    if spectra_bytes <= 4 * 2**20 and green.shape[2] % 8 == 0 and lax.axis_size("slab") % 4 == 0:
        return rows_body(dipoles, inv_alpha, row_site, green)
    return planes_body(dipoles, inv_alpha, row_site, green)


def solution(mesh):
    return jax.shard_map(
        body,
        mesh=mesh,
        in_specs=(
            P("rep", "slab", None),
            P("slab", None),
            P(None, "slab"),
            P(None, None, "slab", None),
        ),
        out_specs=P("rep", "slab", None),
        check_vma=False,
    )
```

```python
import functools
import math

import jax
import jax.numpy as jnp
import numpy as np
from jax import lax
from jax.experimental import pallas as pl
from jax.experimental.pallas import tpu as pltpu
from jax.sharding import PartitionSpec as P

NX = 256
NY = 128
NZ = 128
CAP = 2


HIGH = lax.Precision.HIGHEST


def dft_table(count_in, length, count_out, direction_sign):
    index_in = jnp.arange(count_in)[:, None]
    index_out = jnp.arange(count_out)[None, :]
    phase_index = index_in * index_out % length
    angles = phase_index.astype(jnp.float32) * (2.0 * math.pi / length)
    cosine = jnp.cos(angles)
    sine_part = jnp.sin(angles) * direction_sign
    factor = 1.0 if direction_sign < 0 else 1.0 / length
    upper_rows = jnp.concatenate([cosine, sine_part], axis=1)
    lower_rows = jnp.concatenate([-sine_part, cosine], axis=1)
    return jnp.concatenate([upper_rows, lower_rows], axis=0) * factor


def middle_transform(values, count_in, length, count_out, direction_sign, pattern):
    index_out = jnp.arange(count_out)[:, None]
    index_in = jnp.arange(count_in)[None, :]
    angles = (index_out * index_in % length).astype(jnp.float32) * (2.0 * math.pi / length)
    factor = 1.0 if direction_sign < 0 else 1.0 / length
    cosine = jnp.cos(angles) * factor
    sine_part = jnp.sin(angles) * (direction_sign * factor)
    mixed_cos = jnp.einsum(pattern, cosine, values, precision=HIGH)
    mixed_sin = jnp.einsum(pattern, sine_part, values, precision=HIGH)
    half_width = values.shape[-1] // 2
    real_part = mixed_cos[..., :half_width] - mixed_sin[..., half_width:]
    imag_part = mixed_cos[..., half_width:] + mixed_sin[..., :half_width]
    return jnp.concatenate([real_part, imag_part], axis=-1)


def apply_kernel(spectrum, green):
    half_width = spectrum.shape[-1] // 2
    sym_index = ((0, 1, 2), (1, 3, 4), (2, 4, 5))
    results = []
    for vector in range(2):
        for target in range(3):
            total_re = jnp.zeros(spectrum.shape[1:-1] + (half_width,), jnp.float32)
            total_im = jnp.zeros(spectrum.shape[1:-1] + (half_width,), jnp.float32)
            for other in range(3):
                kernel = green[sym_index[target][other]]
                source = spectrum[vector * 3 + other]
                kern_re, kern_im = (kernel[..., :half_width], kernel[..., half_width:])
                src_re, src_im = (source[..., :half_width], source[..., half_width:])
                total_re = total_re + kern_re * src_re - kern_im * src_im
                total_im = total_im + kern_re * src_im + kern_im * src_re
            results.append(jnp.concatenate([total_re, total_im], axis=-1))
    return jnp.stack(results, axis=0)


def planes_body(dipoles, inv_alpha, row_site, green):
    devices = lax.axis_size("slab")
    row_len = dipoles.shape[2] // 2
    planes = NZ // 2 // devices
    half_y = NY // 2
    half_z = NZ // 2
    occupied = row_site[0] >= 0
    dest_dev = jnp.where(occupied, row_site[1] // planes, -1)
    local_pos = row_site[1] % planes * half_y + row_site[0]
    slots_all = devices * CAP
    owner_hot = (dest_dev[:, None] == jnp.arange(devices)[None, :]).astype(jnp.int32)
    earlier = jnp.cumsum(owner_hot, axis=0) - owner_hot
    slot_index = jnp.sum(earlier * owner_hot, axis=1)
    target = jnp.where(occupied, dest_dev * CAP + slot_index, -1)
    packer = target[None, :] == jnp.arange(slots_all)[:, None]
    pack_float = packer.astype(jnp.float32)
    send_rows = jnp.einsum("qr,vrx->vqx", pack_float, dipoles, precision=HIGH)
    send_pos = jnp.sum(jnp.where(packer, local_pos[None, :] + 1, 0), axis=1) - 1
    send_pos = send_pos.astype(jnp.float32)[None, :]
    recv_rows, recv_pos = (
        lax.all_to_all(send_rows, "slab", split_axis=1, concat_axis=1, tiled=True),
        lax.all_to_all(send_pos, "slab", split_axis=1, concat_axis=1, tiled=True),
    )
    table_x = dft_table(row_len, NX, NX, -1)
    spectral_rows = jnp.einsum("vqx,xk->vqk", recv_rows, table_x, precision=HIGH)
    plane_cells = planes * half_y
    placer = (recv_pos[0].astype(jnp.int32)[None, :] == jnp.arange(plane_cells)[:, None]).astype(
        jnp.float32
    )
    plane_grid = jnp.einsum("cq,vqk->vck", placer, spectral_rows, precision=HIGH)
    plane_grid = plane_grid.reshape(6, planes, half_y, 2 * NX)
    y_spectrum = middle_transform(plane_grid, half_y, NY, NY, -1, "ky,vzyx->vzkx")
    z_spectrum = middle_transform(
        lax.all_to_all(y_spectrum, "slab", split_axis=2, concat_axis=1, tiled=True),
        half_z,
        NZ,
        NZ,
        -1,
        "kz,vzyx->vkyx",
    )
    image = apply_kernel(z_spectrum, green)
    z_back = middle_transform(image, NZ, NZ, half_z, 1, "kz,vzyx->vkyx")
    fields = middle_transform(
        lax.all_to_all(z_back, "slab", split_axis=1, concat_axis=2, tiled=True),
        NY,
        NY,
        half_y,
        1,
        "ky,vzyx->vzkx",
    )
    flat_fields = fields.reshape(6, plane_cells, 2 * NX)
    picked = jnp.einsum("cq,vck->vqk", placer, flat_fields, precision=HIGH)
    table_back = dft_table(NX, NX, row_len, 1)
    back_rows = jnp.einsum("vqk,kx->vqx", picked, table_back, precision=HIGH)
    returned = jnp.einsum(
        "qr,vqx->vrx",
        pack_float,
        lax.all_to_all(back_rows, "slab", split_axis=1, concat_axis=1, tiled=True),
        precision=HIGH,
    )
    row_mask = occupied.astype(jnp.float32)[None, :, None]
    alpha_re = inv_alpha[:, :row_len]
    alpha_im = inv_alpha[:, row_len:]
    dip_re = dipoles[:, :, :row_len]
    dip_im = dipoles[:, :, row_len:]
    out_re = alpha_re * dip_re - alpha_im * dip_im - returned[:, :, :row_len]
    out_im = alpha_re * dip_im + alpha_im * dip_re - returned[:, :, row_len:]
    return jnp.concatenate([out_re, out_im], axis=-1) * row_mask


BF = jnp.bfloat16
F32 = jnp.float32
SYM = ((0, 1, 2), (1, 3, 4), (2, 4, 5))


def split(values):
    high = values.astype(BF)
    return high, (values - high.astype(F32)).astype(BF)


def left3(values):
    high, low = split(values)
    return jnp.concatenate([high, high, low], axis=1)


def right3(values):
    high, low = split(values)
    return jnp.concatenate([high, low, high], axis=0)


def mm(left, right):
    return jnp.dot(left, right, preferred_element_type=F32)


def trig(rows, cols, length):
    angles = 2.0 * np.pi * (np.arange(rows)[:, None] * np.arange(cols)[None, :] % length) / length
    return np.cos(angles), np.sin(angles)


def stack3(table):
    return right3(jnp.asarray(table.astype(np.float32)))


def spectral_kernel(
    rows_ref, green_ref, ty_ref, tz_ref, tx_ref, tb_ref, out_ref,
    xs, ez, ey, spec, img, acc,
):
    step = pl.program_id(0)
    steps = pl.num_programs(0)
    n_dev, comps, per_dev, width = out_ref.shape
    n_rows = n_dev * per_dev
    kz_block, ky_count = green_ref.shape[1], green_ref.shape[2]
    nx = green_ref.shape[3] // 2
    cells = kz_block * ky_count

    @pl.when(step == 0)
    def _():
        acc[...] = jnp.zeros_like(acc)
        sites = rows_ref[:, comps].reshape(n_rows, width)
        for axis, (table, dest) in enumerate(((ty_ref, ey), (tz_ref, ez))):
            half = table.shape[2]
            column = sites[:, axis : axis + 1].astype(jnp.int32)
            hot = (lax.broadcasted_iota(jnp.int32, (n_rows, half), 1) == column).astype(F32)
            for part in range(2):
                dest[part] = lax.dot_general(
                    table[part], hot, (((1,), (1,)), ((), ())), precision=HIGH, preferred_element_type=F32
                )
        for c in range(comps):
            rows = rows_ref[:, c].reshape(n_rows, width)
            x = mm(left3(rows), tx_ref[...])
            x_re, x_im = x[:, :nx], x[:, nx:]
            xs[0, c] = right3(x_re)
            xs[1, c] = right3(x_im)
            xs[2, c] = right3(x_re + x_im)

    zc = ez[0, pl.ds(step * kz_block, kz_block), :][:, None, :]
    zs = ez[1, pl.ds(step * kz_block, kz_block), :][:, None, :]
    yc = ey[0][None]
    ys = ey[1][None]
    a = (zc * yc - zs * ys).reshape(cells, n_rows)
    b = -(zc * ys + zs * yc).reshape(cells, n_rows)
    fa, fb, fab = left3(a), left3(b), left3(a + b)
    for c in range(comps):
        p1 = mm(fa, xs[0, c])
        p2 = mm(fb, xs[1, c])
        p3 = mm(fab, xs[2, c])
        spec[c, 0] = p1 - p2
        spec[c, 1] = p3 - p1 - p2

    a_t = a.T
    b_t = -b.T
    ga, gb, gab = left3(a_t), left3(b_t), left3(a_t + b_t)

    kz_chunk = max(1, 16 // ky_count)
    chunk = kz_chunk * ky_count

    def apply_chunk(j, carry):
        row = pl.multiple_of(j * chunk, chunk)
        for lane in range(0, nx, 128):
            g = [
                [
                    green_ref[m, pl.ds(j * kz_chunk, kz_chunk), :, pl.ds(part * nx + lane, 128)].reshape(chunk, 128)
                    for part in range(2)
                ]
                for m in range(6)
            ]
            for v in range(comps // 3):
                s = [[spec[3 * v + o, part, pl.ds(row, chunk), pl.ds(lane, 128)] for part in range(2)] for o in range(3)]
                for t in range(3):
                    re = im = None
                    for o in range(3):
                        k_re, k_im = g[SYM[t][o]]
                        s_re, s_im = s[o]
                        d_re = k_re * s_re - k_im * s_im
                        d_im = k_re * s_im + k_im * s_re
                        re = d_re if re is None else re + d_re
                        im = d_im if im is None else im + d_im
                    for kind, value in enumerate((re, im, re + im)):
                        high, low = split(value)
                        img[kind, 3 * v + t, 0, pl.ds(row, chunk), pl.ds(lane, 128)] = high
                        img[kind, 3 * v + t, 1, pl.ds(row, chunk), pl.ds(lane, 128)] = low
        return carry

    lax.fori_loop(0, kz_block // kz_chunk, apply_chunk, 0)

    for c in range(comps):
        for kind, left in enumerate((ga, gb, gab)):
            high = img[kind, c, 0]
            low = img[kind, c, 1]
            acc[kind, c] += mm(left, jnp.concatenate([high, low, high], axis=0))

    @pl.when(step == steps - 1)
    def _():
        for c in range(comps):
            p1, p2, p3 = acc[0, c], acc[1, c], acc[2, c]
            both = jnp.concatenate([p1 - p2, p3 - p1 - p2], axis=1)
            out_ref[:, c] = mm(left3(both), tb_ref[...]).reshape(n_dev, per_dev, width)


def spectral(rows, green, nx, ny, nz):
    n_dev, planes, per_dev, width = rows.shape
    comps = planes - 1
    n_rows = n_dev * per_dev
    ky_count = green.shape[2]
    row_len = width // 2
    kz_block = 256 // ky_count
    cos_x, sin_x = trig(row_len, nx, nx)
    forward_x = np.block([[cos_x, -sin_x], [sin_x, cos_x]])
    back_x = np.block([[cos_x.T, sin_x.T], [-sin_x.T, cos_x.T]]) / float(nx * ny * nz)
    table_y = jnp.asarray(np.stack(trig(ny, ny // 2, ny)).astype(np.float32))
    table_y = lax.dynamic_slice_in_dim(table_y, lax.axis_index("slab") * ky_count, ky_count, 1)
    table_z = jnp.asarray(np.stack(trig(nz, nz // 2, nz)).astype(np.float32))
    whole = lambda: pl.BlockSpec(memory_space=pltpu.VMEM)
    return pl.pallas_call(
        spectral_kernel,
        grid=(nz // kz_block,),
        out_shape=jax.ShapeDtypeStruct((n_dev, comps, per_dev, width), F32),
        in_specs=[
            whole(),
            pl.BlockSpec((6, kz_block, ky_count, 2 * nx), lambda i: (0, i, 0, 0)),
            whole(),
            whole(),
            whole(),
            whole(),
        ],
        out_specs=pl.BlockSpec(memory_space=pltpu.VMEM),
        scratch_shapes=[
            pltpu.VMEM((3, comps, 3 * n_rows, nx), BF),
            pltpu.VMEM((2, nz, n_rows), F32),
            pltpu.VMEM((2, ky_count, n_rows), F32),
            pltpu.VMEM((comps, 2, kz_block * ky_count, nx), F32),
            pltpu.VMEM((3, comps, 2, kz_block * ky_count, nx), BF),
            pltpu.VMEM((3, comps, n_rows, nx), F32),
        ],
        compiler_params=pltpu.CompilerParams(vmem_limit_bytes=60000 * 1024),
    )(rows, green, table_y, table_z, stack3(forward_x), stack3(back_x))


def place(n_dev):
    me = lax.axis_index("slab")
    return me, me // 4, (me // 2) % 2, me % 2, n_dev // 4


def slot_of(z, x, core):
    return (z * 2 + x) * 2 + core


def greet(peers):
    barrier = pltpu.get_barrier_semaphore()
    for peer in peers:
        pl.semaphore_signal(barrier, inc=1, device_id={"slab": peer}, device_id_type=pl.DeviceIdType.MESH)
    pl.semaphore_wait(barrier, len(peers))


def send(src, dst, send_sem, recv_sem, peer):
    copy = pltpu.make_async_remote_copy(
        src_ref=src,
        dst_ref=dst,
        send_sem=send_sem,
        recv_sem=recv_sem,
        device_id={"slab": peer},
        device_id_type=pl.DeviceIdType.MESH,
    )
    copy.start()
    return copy


def site_columns(site_ref):
    per_dev = site_ref.shape[1]
    row = lax.broadcasted_iota(jnp.int32, (per_dev, per_dev), 0)
    col = lax.broadcasted_iota(jnp.int32, (per_dev, per_dev), 1)
    return [
        jnp.sum(jnp.where(row == col, site_ref[axis : axis + 1, :].astype(F32), 0.0), axis=1, keepdims=True)
        for axis in range(2)
    ]


CHUNKS = 2


class Sender:
    def __init__(self, send_sems, recv_sems):
        self.send_sems, self.recv_sems = send_sems, recv_sems
        self.copies = {}

    def start(self, key, src, dst, peer):
        k = len(self.copies)
        self.copies[key] = send(src, dst, self.send_sems.at[k], self.recv_sems.at[k], peer)

    def arrived(self, key):
        self.copies[key].wait_recv()

    def sent(self):
        for copy in self.copies.values():
            copy.wait_send()


def gather_kernel(dip_ref, site_ref, all_ref, send_sems, recv_sems):
    n_dev = all_ref.shape[0]
    comps, per_dev, width = dip_ref.shape
    me, z, x, core, depth = place(n_dev)
    half = depth // 2
    all_ref[me, pl.ds(0, comps)] = dip_ref[...]
    y_col, z_col = site_columns(site_ref)
    lane = lax.broadcasted_iota(jnp.int32, (per_dev, width), 1)
    all_ref[me, comps] = jnp.where(lane == 0, y_col, z_col)
    at_z = lambda d, col: slot_of((z + d + depth) % depth, col, core)
    x_peer, c_peer = slot_of(z, 1 - x, core), slot_of(z, x, 1 - core)
    greet([x_peer, c_peer, at_z(1, x), at_z(-1, x)])
    way = 1 - 2 * core
    net = Sender(send_sems, recv_sems)
    span = comps // CHUNKS
    pieces = [(q * span, span if q < CHUNKS - 1 else comps + 1 - q * span) for q in range(CHUNKS)]

    def pass_on(kind, q, d, col, peer):
        lo, count = pieces[q]
        piece = all_ref.at[at_z(-d, x if col == 0 else 1 - x), pl.ds(lo, count)]
        net.start((kind, q, d, col), piece, piece, peer)

    for q in range(CHUNKS):
        pass_on("x", q, 0, 0, x_peer)
        for s in (1, -1):
            pass_on(s, q, 0, 0, at_z(s, x))
    for q in range(CHUNKS):
        pass_on("c", q, 0, 0, c_peer)
    for k in range(1, half + 1):
        for q in range(CHUNKS):
            if k < half:
                for s in (1, -1):
                    net.arrived((s, q, s * (k - 1), 0))
                if k + 1 < half:
                    for s in (1, -1):
                        pass_on(s, q, s * k, 0, at_z(s, x))
                else:
                    lo, count = pieces[q]
                    piece = all_ref.at[at_z(-way * k, x), pl.ds(lo, count)]
                    net.start(("h", q), piece, piece, at_z(way, x))
                for s in (1, -1):
                    pass_on("c", q, s * k, 0, c_peer)
                if k == 1:
                    net.arrived(("x", q, 0, 0))
                    for s in (1, -1):
                        pass_on(s, q, 0, 1, at_z(s, x))
                    pass_on("c", q, 0, 1, c_peer)
            else:
                net.arrived(("h", q))
                pass_on("x", q, half, 0, x_peer)
                pass_on("c", q, half, 0, c_peer)
    for k in range(1, half):
        for q in range(CHUNKS):
            for s in (1, -1):
                net.arrived((s, q, s * (k - 1), 1))
                if k + 1 < half:
                    pass_on(s, q, s * k, 1, at_z(s, x))
                pass_on("c", q, s * k, 1, c_peer)
    for q in range(CHUNKS):
        net.arrived(("x", q, half, 0))
        pass_on("c", q, half, 1, c_peer)
    for key in net.copies:
        if key[0] == "c":
            net.arrived(key)
    net.sent()


def gather_rows(dipoles, row_site):
    n_dev = lax.axis_size("slab")
    comps, per_dev, width = dipoles.shape
    count = CHUNKS * 2 * n_dev
    return pl.pallas_call(
        gather_kernel,
        out_shape=jax.ShapeDtypeStruct((n_dev, comps + 1, per_dev, width), F32),
        in_specs=[pl.BlockSpec(memory_space=pltpu.VMEM)] * 2,
        out_specs=pl.BlockSpec(memory_space=pltpu.VMEM),
        scratch_shapes=[pltpu.SemaphoreType.DMA((count,)), pltpu.SemaphoreType.DMA((count,))],
        compiler_params=pltpu.CompilerParams(collective_id=0, has_side_effects=True),
    )(dipoles, row_site)


def reduce_kernel(part_ref, dip_ref, alpha_ref, site_ref, out_ref, got_c, got, total, send_sems, recv_sems):
    n_dev, comps, per_dev, width = part_ref.shape
    row_len = width // 2
    me, z, x, core, depth = place(n_dev)
    half = depth // 2
    at_z = lambda d, col: slot_of((z + d + depth) % depth, col, core)
    x_peer, c_peer = slot_of(z, 1 - x, core), slot_of(z, x, 1 - core)
    greet([x_peer, c_peer, at_z(1, x), at_z(-1, x)])
    way = 1 - 2 * core
    net = Sender(send_sems, recv_sems)
    span = comps // CHUNKS
    col_of = lambda col: x if col == 0 else 1 - x
    offsets = [d for k in range(half - 1, 0, -1) for d in (k, -k)]
    order = [(half, 1), *((d, 1) for d in offsets), (half, 0), *((d, 0) for d in offsets), (0, 1), (0, 0)]
    got_at = {}

    def piece(ref, q):
        return ref.at[pl.ds(q * span, span)]

    def move(kind, q, d, col, peer):
        at = got_at.setdefault((kind, d, col), len(got_at))
        net.start((kind, q, d, col), piece(total.at[order.index((d, col))], q), piece(got.at[at], q), peer)

    def add(q, d, col, *keys):
        chunk = pl.ds(q * span, span)
        value = total[order.index((d, col)), chunk]
        for kind, from_d, from_col in keys:
            net.arrived((kind, q, from_d, from_col))
            value = value + got[got_at[kind, from_d, from_col], chunk]
        total[order.index((d, col)), chunk] = value

    for q in range(CHUNKS):
        for k, (d, col) in enumerate(order):
            slot = slot_of((z + d + depth) % depth, col_of(col), 1 - core)
            net.start(("c", q, d, col), piece(part_ref.at[slot], q), piece(got_c.at[k], q), c_peer)

    def both_cores(q, d, col):
        net.arrived(("c", q, d, col))
        k = order.index((d, col))
        chunk = pl.ds(q * span, span)
        total[k, chunk] = part_ref[at_z(d, col_of(col)), chunk] + got_c[k, chunk]

    for q in range(CHUNKS):
        both_cores(q, half, 1)
        move("x", q, half, 1, x_peer)
        for d in offsets:
            both_cores(q, d, 1)
            if abs(d) == half - 1:
                move("z", q, d, 1, at_z(1 if d > 0 else -1, x))
    for k in range(half - 2, 0, -1):
        for q in range(CHUNKS):
            for d in (k, -k):
                add(q, d, 1, ("z", d + (1 if d > 0 else -1), 1))
                move("z", q, d, 1, at_z(1 if d > 0 else -1, x))
    for q in range(CHUNKS):
        both_cores(q, half, 0)
        add(q, half, 0, ("x", half, 1))
        at = got_at.setdefault("h", len(got_at))
        net.start(("h", q), piece(total.at[order.index((half, 0))], q), piece(got.at[at], q), at_z(way, x))
        for d in (0, *offsets):
            both_cores(q, d, 1 if d == 0 else 0)
        add(q, 0, 1, ("z", 1, 1), ("z", -1, 1))
        move("x", q, 0, 1, x_peer)
    for k in range(half - 1, 0, -1):
        for q in range(CHUNKS):
            for d in (k, -k):
                s = 1 if d > 0 else -1
                if k == half - 1:
                    if d > 0:
                        net.arrived(("h", q))
                    chunk = pl.ds(q * span, span)
                    index = order.index((d, 0))
                    extra = jnp.where(way == s, got[got_at["h"], chunk], 0.0)
                    total[index, chunk] = total[index, chunk] + extra
                else:
                    add(q, d, 0, ("z", d + s, 0))
                move("z", q, d, 0, at_z(s, x))
    a_re, a_im = alpha_ref[:, :row_len], alpha_ref[:, row_len:]
    y_col, _ = site_columns(site_ref)
    live = y_col >= 0.0
    own = order.index((0, 0))
    for q in range(CHUNKS):
        both_cores(q, 0, 0)
        add(q, 0, 0, ("x", 0, 1), ("z", 1, 0), ("z", -1, 0))
        for c in range(q * span, (q + 1) * span):
            v_re, v_im = total[own, c, :, :row_len], total[own, c, :, row_len:]
            d_re, d_im = dip_ref[c, :, :row_len], dip_ref[c, :, row_len:]
            o_re = a_re * d_re - a_im * d_im - v_re
            o_im = a_re * d_im + a_im * d_re - v_im
            out_ref[c] = jnp.where(live, jnp.concatenate([o_re, o_im], axis=1), 0.0)
    net.sent()


def reduce_rows(partial, dipoles, inv_alpha, row_site):
    n_dev, *block = partial.shape
    count = CHUNKS * 2 * n_dev
    hold = lambda slots: pltpu.VMEM((slots, *block), F32)
    return pl.pallas_call(
        reduce_kernel,
        out_shape=jax.ShapeDtypeStruct(dipoles.shape, F32),
        in_specs=[pl.BlockSpec(memory_space=pltpu.VMEM)] * 4,
        out_specs=pl.BlockSpec(memory_space=pltpu.VMEM),
        scratch_shapes=[
            hold(n_dev // 2), hold(n_dev // 2), hold(n_dev // 2),
            pltpu.SemaphoreType.DMA((count,)), pltpu.SemaphoreType.DMA((count,)),
        ],
        compiler_params=pltpu.CompilerParams(collective_id=1, has_side_effects=True),
    )(partial, dipoles, inv_alpha, row_site)


def rows_body(dipoles, inv_alpha, row_site, green):
    nz = green.shape[1]
    nx = green.shape[3] // 2
    ny = green.shape[2] * lax.axis_size("slab")
    rows = gather_rows(dipoles, row_site)
    partial = spectral(rows, green, nx, ny, nz)
    return reduce_rows(partial, dipoles, inv_alpha, row_site)


def body(dipoles, inv_alpha, row_site, green):
    n_rows = dipoles.shape[1] * lax.axis_size("slab")
    spectra_bytes = 4 * dipoles.shape[0] * n_rows * green.shape[3]
    if spectra_bytes <= 4 * 2**20 and green.shape[2] % 8 == 0 and lax.axis_size("slab") % 16 == 0:
        return rows_body(dipoles, inv_alpha, row_site, green)
    return planes_body(dipoles, inv_alpha, row_site, green)


def solution(mesh):
    return jax.shard_map(
        body,
        mesh=mesh,
        in_specs=(
            P("rep", "slab", None),
            P("slab", None),
            P(None, "slab"),
            P(None, None, "slab", None),
        ),
        out_specs=P("rep", "slab", None),
        check_vma=False,
    )
```

```python
import functools
import math

import jax
import jax.numpy as jnp
import numpy as np
from jax import lax
from jax.experimental import pallas as pl
from jax.experimental.pallas import tpu as pltpu
from jax.sharding import PartitionSpec as P

NX = 256
NY = 128
NZ = 128
CAP = 2


HIGH = lax.Precision.HIGHEST


def dft_table(count_in, length, count_out, direction_sign):
    index_in = jnp.arange(count_in)[:, None]
    index_out = jnp.arange(count_out)[None, :]
    phase_index = index_in * index_out % length
    angles = phase_index.astype(jnp.float32) * (2.0 * math.pi / length)
    cosine = jnp.cos(angles)
    sine_part = jnp.sin(angles) * direction_sign
    factor = 1.0 if direction_sign < 0 else 1.0 / length
    upper_rows = jnp.concatenate([cosine, sine_part], axis=1)
    lower_rows = jnp.concatenate([-sine_part, cosine], axis=1)
    return jnp.concatenate([upper_rows, lower_rows], axis=0) * factor


def middle_transform(values, count_in, length, count_out, direction_sign, pattern):
    index_out = jnp.arange(count_out)[:, None]
    index_in = jnp.arange(count_in)[None, :]
    angles = (index_out * index_in % length).astype(jnp.float32) * (2.0 * math.pi / length)
    factor = 1.0 if direction_sign < 0 else 1.0 / length
    cosine = jnp.cos(angles) * factor
    sine_part = jnp.sin(angles) * (direction_sign * factor)
    mixed_cos = jnp.einsum(pattern, cosine, values, precision=HIGH)
    mixed_sin = jnp.einsum(pattern, sine_part, values, precision=HIGH)
    half_width = values.shape[-1] // 2
    real_part = mixed_cos[..., :half_width] - mixed_sin[..., half_width:]
    imag_part = mixed_cos[..., half_width:] + mixed_sin[..., :half_width]
    return jnp.concatenate([real_part, imag_part], axis=-1)


def apply_kernel(spectrum, green):
    half_width = spectrum.shape[-1] // 2
    sym_index = ((0, 1, 2), (1, 3, 4), (2, 4, 5))
    results = []
    for vector in range(2):
        for target in range(3):
            total_re = jnp.zeros(spectrum.shape[1:-1] + (half_width,), jnp.float32)
            total_im = jnp.zeros(spectrum.shape[1:-1] + (half_width,), jnp.float32)
            for other in range(3):
                kernel = green[sym_index[target][other]]
                source = spectrum[vector * 3 + other]
                kern_re, kern_im = (kernel[..., :half_width], kernel[..., half_width:])
                src_re, src_im = (source[..., :half_width], source[..., half_width:])
                total_re = total_re + kern_re * src_re - kern_im * src_im
                total_im = total_im + kern_re * src_im + kern_im * src_re
            results.append(jnp.concatenate([total_re, total_im], axis=-1))
    return jnp.stack(results, axis=0)


def planes_body(dipoles, inv_alpha, row_site, green):
    devices = lax.axis_size("slab")
    row_len = dipoles.shape[2] // 2
    planes = NZ // 2 // devices
    half_y = NY // 2
    half_z = NZ // 2
    occupied = row_site[0] >= 0
    dest_dev = jnp.where(occupied, row_site[1] // planes, -1)
    local_pos = row_site[1] % planes * half_y + row_site[0]
    slots_all = devices * CAP
    owner_hot = (dest_dev[:, None] == jnp.arange(devices)[None, :]).astype(jnp.int32)
    earlier = jnp.cumsum(owner_hot, axis=0) - owner_hot
    slot_index = jnp.sum(earlier * owner_hot, axis=1)
    target = jnp.where(occupied, dest_dev * CAP + slot_index, -1)
    packer = target[None, :] == jnp.arange(slots_all)[:, None]
    pack_float = packer.astype(jnp.float32)
    send_rows = jnp.einsum("qr,vrx->vqx", pack_float, dipoles, precision=HIGH)
    send_pos = jnp.sum(jnp.where(packer, local_pos[None, :] + 1, 0), axis=1) - 1
    send_pos = send_pos.astype(jnp.float32)[None, :]
    recv_rows, recv_pos = (
        lax.all_to_all(send_rows, "slab", split_axis=1, concat_axis=1, tiled=True),
        lax.all_to_all(send_pos, "slab", split_axis=1, concat_axis=1, tiled=True),
    )
    table_x = dft_table(row_len, NX, NX, -1)
    spectral_rows = jnp.einsum("vqx,xk->vqk", recv_rows, table_x, precision=HIGH)
    plane_cells = planes * half_y
    placer = (recv_pos[0].astype(jnp.int32)[None, :] == jnp.arange(plane_cells)[:, None]).astype(
        jnp.float32
    )
    plane_grid = jnp.einsum("cq,vqk->vck", placer, spectral_rows, precision=HIGH)
    plane_grid = plane_grid.reshape(6, planes, half_y, 2 * NX)
    y_spectrum = middle_transform(plane_grid, half_y, NY, NY, -1, "ky,vzyx->vzkx")
    z_spectrum = middle_transform(
        lax.all_to_all(y_spectrum, "slab", split_axis=2, concat_axis=1, tiled=True),
        half_z,
        NZ,
        NZ,
        -1,
        "kz,vzyx->vkyx",
    )
    image = apply_kernel(z_spectrum, green)
    z_back = middle_transform(image, NZ, NZ, half_z, 1, "kz,vzyx->vkyx")
    fields = middle_transform(
        lax.all_to_all(z_back, "slab", split_axis=1, concat_axis=2, tiled=True),
        NY,
        NY,
        half_y,
        1,
        "ky,vzyx->vzkx",
    )
    flat_fields = fields.reshape(6, plane_cells, 2 * NX)
    picked = jnp.einsum("cq,vck->vqk", placer, flat_fields, precision=HIGH)
    table_back = dft_table(NX, NX, row_len, 1)
    back_rows = jnp.einsum("vqk,kx->vqx", picked, table_back, precision=HIGH)
    returned = jnp.einsum(
        "qr,vqx->vrx",
        pack_float,
        lax.all_to_all(back_rows, "slab", split_axis=1, concat_axis=1, tiled=True),
        precision=HIGH,
    )
    row_mask = occupied.astype(jnp.float32)[None, :, None]
    alpha_re = inv_alpha[:, :row_len]
    alpha_im = inv_alpha[:, row_len:]
    dip_re = dipoles[:, :, :row_len]
    dip_im = dipoles[:, :, row_len:]
    out_re = alpha_re * dip_re - alpha_im * dip_im - returned[:, :, :row_len]
    out_im = alpha_re * dip_im + alpha_im * dip_re - returned[:, :, row_len:]
    return jnp.concatenate([out_re, out_im], axis=-1) * row_mask


BF = jnp.bfloat16
F32 = jnp.float32
SYM = ((0, 1, 2), (1, 3, 4), (2, 4, 5))


def split(values):
    high = values.astype(BF)
    return high, (values - high.astype(F32)).astype(BF)


def left3(values):
    high, low = split(values)
    return jnp.concatenate([high, high, low], axis=1)


def right3(values):
    high, low = split(values)
    return jnp.concatenate([high, low, high], axis=0)


def mm(left, right):
    return jnp.dot(left, right, preferred_element_type=F32)


def trig(rows, cols, length):
    angles = 2.0 * np.pi * (np.arange(rows)[:, None] * np.arange(cols)[None, :] % length) / length
    return np.cos(angles), np.sin(angles)


def stack3(table):
    return right3(jnp.asarray(table.astype(np.float32)))


def spectral_kernel(
    rows_ref, green_ref, ty_ref, tz_ref, tx_ref, tb_ref, out_ref,
    xs, ez, ey, spec, img, acc,
):
    step = pl.program_id(0)
    steps = pl.num_programs(0)
    n_dev, comps, per_dev, width = out_ref.shape
    n_rows = n_dev * per_dev
    kz_block, ky_count = green_ref.shape[1], green_ref.shape[2]
    nx = green_ref.shape[3] // 2
    cells = kz_block * ky_count

    @pl.when(step == 0)
    def _():
        acc[...] = jnp.zeros_like(acc)
        sites = rows_ref[:, comps].reshape(n_rows, width)
        first_ky = pl.multiple_of(lax.axis_index("slab") * ky_count, ky_count)
        for axis, (table, dest, first) in enumerate(((ty_ref, ey, first_ky), (tz_ref, ez, 0))):
            half = table.shape[2]
            column = sites[:, axis : axis + 1].astype(jnp.int32)
            hot = (lax.broadcasted_iota(jnp.int32, (n_rows, half), 1) == column).astype(F32)
            for part in range(2):
                dest[part] = lax.dot_general(
                    table[part, pl.ds(first, dest.shape[1])], hot, (((1,), (1,)), ((), ())), precision=HIGH, preferred_element_type=F32
                )
        for c in range(comps):
            rows = rows_ref[:, c].reshape(n_rows, width)
            x = mm(left3(rows), tx_ref[...])
            x_re, x_im = x[:, :nx], x[:, nx:]
            xs[0, c] = right3(x_re)
            xs[1, c] = right3(x_im)
            xs[2, c] = right3(x_re + x_im)

    zc = ez[0, pl.ds(step * kz_block, kz_block), :][:, None, :]
    zs = ez[1, pl.ds(step * kz_block, kz_block), :][:, None, :]
    yc = ey[0][None]
    ys = ey[1][None]
    a = (zc * yc - zs * ys).reshape(cells, n_rows)
    b = -(zc * ys + zs * yc).reshape(cells, n_rows)
    fa, fb, fab = left3(a), left3(b), left3(a + b)
    for c in range(comps):
        p1 = mm(fa, xs[0, c])
        p2 = mm(fb, xs[1, c])
        p3 = mm(fab, xs[2, c])
        spec[c, 0] = p1 - p2
        spec[c, 1] = p3 - p1 - p2

    a_t = a.T
    b_t = -b.T
    ga, gb, gab = left3(a_t), left3(b_t), left3(a_t + b_t)

    kz_chunk = max(1, 16 // ky_count)
    chunk = kz_chunk * ky_count

    def apply_chunk(j):
        row = j * chunk
        for lane in range(0, nx, 128):
            g = [
                [
                    green_ref[m, pl.ds(j * kz_chunk, kz_chunk), :, pl.ds(part * nx + lane, 128)].reshape(chunk, 128)
                    for part in range(2)
                ]
                for m in range(6)
            ]
            for v in range(comps // 3):
                s = [[spec[3 * v + o, part, pl.ds(row, chunk), pl.ds(lane, 128)] for part in range(2)] for o in range(3)]
                for t in range(3):
                    re = im = None
                    for o in range(3):
                        k_re, k_im = g[SYM[t][o]]
                        s_re, s_im = s[o]
                        d_re = k_re * s_re - k_im * s_im
                        d_im = k_re * s_im + k_im * s_re
                        re = d_re if re is None else re + d_re
                        im = d_im if im is None else im + d_im
                    for kind, value in enumerate((re, im, re + im)):
                        high, low = split(value)
                        img[kind, 3 * v + t, 0, pl.ds(row, chunk), pl.ds(lane, 128)] = high
                        img[kind, 3 * v + t, 1, pl.ds(row, chunk), pl.ds(lane, 128)] = low

    for j in range(kz_block // kz_chunk):
        apply_chunk(j)

    for c in range(comps):
        for kind, left in enumerate((ga, gb, gab)):
            high = img[kind, c, 0]
            low = img[kind, c, 1]
            acc[kind, c] += mm(left, jnp.concatenate([high, low, high], axis=0))

    @pl.when(step == steps - 1)
    def _():
        for c in range(comps):
            p1, p2, p3 = acc[0, c], acc[1, c], acc[2, c]
            both = jnp.concatenate([p1 - p2, p3 - p1 - p2], axis=1)
            out_ref[:, c] = mm(left3(both), tb_ref[...]).reshape(n_dev, per_dev, width)


def spectral(rows, green, nx, ny, nz):
    n_dev, planes, per_dev, width = rows.shape
    comps = planes - 1
    n_rows = n_dev * per_dev
    ky_count = green.shape[2]
    row_len = width // 2
    kz_block = 256 // ky_count
    cos_x, sin_x = trig(row_len, nx, nx)
    forward_x = np.block([[cos_x, -sin_x], [sin_x, cos_x]])
    back_x = np.block([[cos_x.T, sin_x.T], [-sin_x.T, cos_x.T]]) / float(nx * ny * nz)
    table_y = jnp.asarray(np.stack(trig(ny, ny // 2, ny)).astype(np.float32))
    table_z = jnp.asarray(np.stack(trig(nz, nz // 2, nz)).astype(np.float32))
    whole = lambda: pl.BlockSpec(memory_space=pltpu.VMEM)
    return pl.pallas_call(
        spectral_kernel,
        grid=(nz // kz_block,),
        out_shape=jax.ShapeDtypeStruct((n_dev, comps, per_dev, width), F32),
        in_specs=[
            whole(),
            pl.BlockSpec((6, kz_block, ky_count, 2 * nx), lambda i: (0, i, 0, 0)),
            whole(),
            whole(),
            whole(),
            whole(),
        ],
        out_specs=pl.BlockSpec(memory_space=pltpu.VMEM),
        scratch_shapes=[
            pltpu.VMEM((3, comps, 3 * n_rows, nx), BF),
            pltpu.VMEM((2, nz, n_rows), F32),
            pltpu.VMEM((2, ky_count, n_rows), F32),
            pltpu.VMEM((comps, 2, kz_block * ky_count, nx), F32),
            pltpu.VMEM((3, comps, 2, kz_block * ky_count, nx), BF),
            pltpu.VMEM((3, comps, n_rows, nx), F32),
        ],
        compiler_params=pltpu.CompilerParams(vmem_limit_bytes=60000 * 1024),
    )(rows, green, table_y, table_z, stack3(forward_x), stack3(back_x))


def place(n_dev):
    me = lax.axis_index("slab")
    return me, me // 4, (me // 2) % 2, me % 2, n_dev // 4


def slot_of(z, x, core):
    return (z * 2 + x) * 2 + core


def greet(peers):
    barrier = pltpu.get_barrier_semaphore()
    for peer in peers:
        pl.semaphore_signal(barrier, inc=1, device_id={"slab": peer}, device_id_type=pl.DeviceIdType.MESH)
    pl.semaphore_wait(barrier, len(peers))


def send(src, dst, send_sem, recv_sem, peer):
    copy = pltpu.make_async_remote_copy(
        src_ref=src,
        dst_ref=dst,
        send_sem=send_sem,
        recv_sem=recv_sem,
        device_id={"slab": peer},
        device_id_type=pl.DeviceIdType.MESH,
    )
    copy.start()
    return copy


def site_columns(site_ref):
    per_dev = site_ref.shape[1]
    row = lax.broadcasted_iota(jnp.int32, (per_dev, per_dev), 0)
    col = lax.broadcasted_iota(jnp.int32, (per_dev, per_dev), 1)
    return [
        jnp.sum(jnp.where(row == col, site_ref[axis : axis + 1, :].astype(F32), 0.0), axis=1, keepdims=True)
        for axis in range(2)
    ]


CHUNKS = 2


class Sender:
    def __init__(self, send_sems, recv_sems):
        self.send_sems, self.recv_sems = send_sems, recv_sems
        self.copies = {}

    def start(self, key, src, dst, peer):
        k = len(self.copies)
        self.copies[key] = send(src, dst, self.send_sems.at[k], self.recv_sems.at[k], peer)

    def arrived(self, key):
        self.copies[key].wait_recv()

    def sent(self):
        for copy in self.copies.values():
            copy.wait_send()


def gather_kernel(dip_ref, site_ref, all_ref, send_z, recv_z, send_x, recv_x, send_c, recv_c):
    n_dev = all_ref.shape[0]
    comps, per_dev, width = dip_ref.shape
    me, z, x, core, depth = place(n_dev)
    all_ref[me, pl.ds(0, comps)] = dip_ref[...]
    y_col, z_col = site_columns(site_ref)
    lane = lax.broadcasted_iota(jnp.int32, (per_dev, width), 1)
    all_ref[me, comps] = jnp.where(lane == 0, y_col, z_col)
    x_peer, c_peer = slot_of(z, 1 - x, core), slot_of(z, x, 1 - core)
    greet([x_peer, c_peer, *(slot_of((z + d) % depth, x, core) for d in range(1, depth))])
    order = sorted(range(1, depth), key=lambda d: min(d, depth - d))
    zs, xs, cs = {}, {}, {}
    for d in order:
        zs[d] = send(all_ref.at[me], all_ref.at[me], send_z.at[d], recv_z.at[d], slot_of((z + d) % depth, x, core))

    def pass_on(d):
        slot = all_ref.at[slot_of((z - d + depth) % depth, x, core)]
        xs[d] = send(slot, slot, send_x.at[d], recv_x.at[d], x_peer)
        cs[d, 0] = send(slot, slot, send_c.at[d], recv_c.at[d], c_peer)

    def cross(d):
        xs[d].wait_recv()
        slot = all_ref.at[slot_of((z - d + depth) % depth, 1 - x, core)]
        cs[d, 1] = send(slot, slot, send_c.at[depth + d], recv_c.at[depth + d], c_peer)

    pass_on(0)
    before = 0
    for d in order:
        zs[d].wait_recv()
        pass_on(d)
        cross(before)
        before = d
    cross(before)
    for copy in cs.values():
        copy.wait_recv()
    for copy in [*zs.values(), *xs.values(), *cs.values()]:
        copy.wait_send()


def gather_rows(dipoles, row_site):
    n_dev = lax.axis_size("slab")
    depth = n_dev // 4
    comps, per_dev, width = dipoles.shape
    dma = pltpu.SemaphoreType.DMA
    return pl.pallas_call(
        gather_kernel,
        out_shape=jax.ShapeDtypeStruct((n_dev, comps + 1, per_dev, width), F32),
        in_specs=[pl.BlockSpec(memory_space=pltpu.VMEM)] * 2,
        out_specs=pl.BlockSpec(memory_space=pltpu.VMEM),
        scratch_shapes=[dma((depth,)), dma((depth,)), dma((depth,)), dma((depth,)), dma((2 * depth,)), dma((2 * depth,))],
        compiler_params=pltpu.CompilerParams(collective_id=0, has_side_effects=True),
    )(dipoles, row_site)


def reduce_kernel(part_ref, dip_ref, alpha_ref, site_ref, out_ref, got_c, got, total, send_sems, recv_sems):
    n_dev, comps, per_dev, width = part_ref.shape
    row_len = width // 2
    me, z, x, core, depth = place(n_dev)
    half = depth // 2
    at_z = lambda d, col: slot_of((z + d + depth) % depth, col, core)
    x_peer, c_peer = slot_of(z, 1 - x, core), slot_of(z, x, 1 - core)
    greet([x_peer, c_peer, at_z(1, x), at_z(-1, x)])
    way = 1 - 2 * core
    net = Sender(send_sems, recv_sems)
    span = comps // CHUNKS
    col_of = lambda col: x if col == 0 else 1 - x
    offsets = [d for k in range(half - 1, 0, -1) for d in (k, -k)]
    order = [(half, 1), *((d, 1) for d in offsets), (half, 0), *((d, 0) for d in offsets), (0, 1), (0, 0)]
    got_at = {}

    def piece(ref, q):
        return ref.at[pl.ds(q * span, span)]

    def move(kind, q, d, col, peer):
        at = got_at.setdefault((kind, d, col), len(got_at))
        net.start((kind, q, d, col), piece(total.at[order.index((d, col))], q), piece(got.at[at], q), peer)

    def add(q, d, col, *keys):
        chunk = pl.ds(q * span, span)
        value = total[order.index((d, col)), chunk]
        for kind, from_d, from_col in keys:
            net.arrived((kind, q, from_d, from_col))
            value = value + got[got_at[kind, from_d, from_col], chunk]
        total[order.index((d, col)), chunk] = value

    for q in range(CHUNKS):
        for k, (d, col) in enumerate(order):
            slot = slot_of((z + d + depth) % depth, col_of(col), 1 - core)
            net.start(("c", q, d, col), piece(part_ref.at[slot], q), piece(got_c.at[k], q), c_peer)

    def both_cores(q, d, col):
        net.arrived(("c", q, d, col))
        k = order.index((d, col))
        chunk = pl.ds(q * span, span)
        total[k, chunk] = part_ref[at_z(d, col_of(col)), chunk] + got_c[k, chunk]

    for q in range(CHUNKS):
        both_cores(q, half, 1)
        move("x", q, half, 1, x_peer)
        for d in offsets:
            both_cores(q, d, 1)
            if abs(d) == half - 1:
                move("z", q, d, 1, at_z(1 if d > 0 else -1, x))
    for k in range(half - 2, 0, -1):
        for q in range(CHUNKS):
            for d in (k, -k):
                add(q, d, 1, ("z", d + (1 if d > 0 else -1), 1))
                move("z", q, d, 1, at_z(1 if d > 0 else -1, x))
    for q in range(CHUNKS):
        both_cores(q, half, 0)
        add(q, half, 0, ("x", half, 1))
        at = got_at.setdefault("h", len(got_at))
        net.start(("h", q), piece(total.at[order.index((half, 0))], q), piece(got.at[at], q), at_z(way, x))
        for d in (0, *offsets):
            both_cores(q, d, 1 if d == 0 else 0)
        add(q, 0, 1, ("z", 1, 1), ("z", -1, 1))
        move("x", q, 0, 1, x_peer)
    for k in range(half - 1, 0, -1):
        for q in range(CHUNKS):
            for d in (k, -k):
                s = 1 if d > 0 else -1
                if k == half - 1:
                    if d > 0:
                        net.arrived(("h", q))
                    chunk = pl.ds(q * span, span)
                    index = order.index((d, 0))
                    extra = jnp.where(way == s, got[got_at["h"], chunk], 0.0)
                    total[index, chunk] = total[index, chunk] + extra
                else:
                    add(q, d, 0, ("z", d + s, 0))
                move("z", q, d, 0, at_z(s, x))
    a_re, a_im = alpha_ref[:, :row_len], alpha_ref[:, row_len:]
    y_col, _ = site_columns(site_ref)
    live = y_col >= 0.0
    own = order.index((0, 0))
    for q in range(CHUNKS):
        both_cores(q, 0, 0)
        add(q, 0, 0, ("x", 0, 1), ("z", 1, 0), ("z", -1, 0))
        for c in range(q * span, (q + 1) * span):
            v_re, v_im = total[own, c, :, :row_len], total[own, c, :, row_len:]
            d_re, d_im = dip_ref[c, :, :row_len], dip_ref[c, :, row_len:]
            o_re = a_re * d_re - a_im * d_im - v_re
            o_im = a_re * d_im + a_im * d_re - v_im
            out_ref[c] = jnp.where(live, jnp.concatenate([o_re, o_im], axis=1), 0.0)
    net.sent()


def reduce_rows(partial, dipoles, inv_alpha, row_site):
    n_dev, *block = partial.shape
    count = CHUNKS * 2 * n_dev
    hold = lambda slots: pltpu.VMEM((slots, *block), F32)
    return pl.pallas_call(
        reduce_kernel,
        out_shape=jax.ShapeDtypeStruct(dipoles.shape, F32),
        in_specs=[pl.BlockSpec(memory_space=pltpu.VMEM)] * 4,
        out_specs=pl.BlockSpec(memory_space=pltpu.VMEM),
        scratch_shapes=[
            hold(n_dev // 2), hold(n_dev // 2), hold(n_dev // 2),
            pltpu.SemaphoreType.DMA((count,)), pltpu.SemaphoreType.DMA((count,)),
        ],
        compiler_params=pltpu.CompilerParams(collective_id=1, has_side_effects=True),
    )(partial, dipoles, inv_alpha, row_site)


def rows_body(dipoles, inv_alpha, row_site, green):
    nz = green.shape[1]
    nx = green.shape[3] // 2
    ny = green.shape[2] * lax.axis_size("slab")
    rows = gather_rows(dipoles, row_site)
    partial = spectral(rows, green, nx, ny, nz)
    return reduce_rows(partial, dipoles, inv_alpha, row_site)


def body(dipoles, inv_alpha, row_site, green):
    n_rows = dipoles.shape[1] * lax.axis_size("slab")
    spectra_bytes = 4 * dipoles.shape[0] * n_rows * green.shape[3]
    if spectra_bytes <= 4 * 2**20 and green.shape[2] % 8 == 0 and lax.axis_size("slab") % 16 == 0:
        return rows_body(dipoles, inv_alpha, row_site, green)
    return planes_body(dipoles, inv_alpha, row_site, green)


def solution(mesh):
    return jax.shard_map(
        body,
        mesh=mesh,
        in_specs=(
            P("rep", "slab", None),
            P("slab", None),
            P(None, "slab"),
            P(None, None, "slab", None),
        ),
        out_specs=P("rep", "slab", None),
        check_vma=False,
    )
```

```python
import functools
import math

import jax
import jax.numpy as jnp
import numpy as np
from jax import lax
from jax.experimental import pallas as pl
from jax.experimental.pallas import tpu as pltpu
from jax.sharding import PartitionSpec as P

NX = 256
NY = 128
NZ = 128
CAP = 2


HIGH = lax.Precision.HIGHEST


def dft_table(count_in, length, count_out, direction_sign):
    index_in = jnp.arange(count_in)[:, None]
    index_out = jnp.arange(count_out)[None, :]
    phase_index = index_in * index_out % length
    angles = phase_index.astype(jnp.float32) * (2.0 * math.pi / length)
    cosine = jnp.cos(angles)
    sine_part = jnp.sin(angles) * direction_sign
    factor = 1.0 if direction_sign < 0 else 1.0 / length
    upper_rows = jnp.concatenate([cosine, sine_part], axis=1)
    lower_rows = jnp.concatenate([-sine_part, cosine], axis=1)
    return jnp.concatenate([upper_rows, lower_rows], axis=0) * factor


def middle_transform(values, count_in, length, count_out, direction_sign, pattern):
    index_out = jnp.arange(count_out)[:, None]
    index_in = jnp.arange(count_in)[None, :]
    angles = (index_out * index_in % length).astype(jnp.float32) * (2.0 * math.pi / length)
    factor = 1.0 if direction_sign < 0 else 1.0 / length
    cosine = jnp.cos(angles) * factor
    sine_part = jnp.sin(angles) * (direction_sign * factor)
    mixed_cos = jnp.einsum(pattern, cosine, values, precision=HIGH)
    mixed_sin = jnp.einsum(pattern, sine_part, values, precision=HIGH)
    half_width = values.shape[-1] // 2
    real_part = mixed_cos[..., :half_width] - mixed_sin[..., half_width:]
    imag_part = mixed_cos[..., half_width:] + mixed_sin[..., :half_width]
    return jnp.concatenate([real_part, imag_part], axis=-1)


def apply_kernel(spectrum, green):
    half_width = spectrum.shape[-1] // 2
    sym_index = ((0, 1, 2), (1, 3, 4), (2, 4, 5))
    results = []
    for vector in range(2):
        for target in range(3):
            total_re = jnp.zeros(spectrum.shape[1:-1] + (half_width,), jnp.float32)
            total_im = jnp.zeros(spectrum.shape[1:-1] + (half_width,), jnp.float32)
            for other in range(3):
                kernel = green[sym_index[target][other]]
                source = spectrum[vector * 3 + other]
                kern_re, kern_im = (kernel[..., :half_width], kernel[..., half_width:])
                src_re, src_im = (source[..., :half_width], source[..., half_width:])
                total_re = total_re + kern_re * src_re - kern_im * src_im
                total_im = total_im + kern_re * src_im + kern_im * src_re
            results.append(jnp.concatenate([total_re, total_im], axis=-1))
    return jnp.stack(results, axis=0)


def planes_body(dipoles, inv_alpha, row_site, green):
    devices = lax.axis_size("slab")
    row_len = dipoles.shape[2] // 2
    planes = NZ // 2 // devices
    half_y = NY // 2
    half_z = NZ // 2
    occupied = row_site[0] >= 0
    dest_dev = jnp.where(occupied, row_site[1] // planes, -1)
    local_pos = row_site[1] % planes * half_y + row_site[0]
    slots_all = devices * CAP
    owner_hot = (dest_dev[:, None] == jnp.arange(devices)[None, :]).astype(jnp.int32)
    earlier = jnp.cumsum(owner_hot, axis=0) - owner_hot
    slot_index = jnp.sum(earlier * owner_hot, axis=1)
    target = jnp.where(occupied, dest_dev * CAP + slot_index, -1)
    packer = target[None, :] == jnp.arange(slots_all)[:, None]
    pack_float = packer.astype(jnp.float32)
    send_rows = jnp.einsum("qr,vrx->vqx", pack_float, dipoles, precision=HIGH)
    send_pos = jnp.sum(jnp.where(packer, local_pos[None, :] + 1, 0), axis=1) - 1
    send_pos = send_pos.astype(jnp.float32)[None, :]
    recv_rows, recv_pos = (
        lax.all_to_all(send_rows, "slab", split_axis=1, concat_axis=1, tiled=True),
        lax.all_to_all(send_pos, "slab", split_axis=1, concat_axis=1, tiled=True),
    )
    table_x = dft_table(row_len, NX, NX, -1)
    spectral_rows = jnp.einsum("vqx,xk->vqk", recv_rows, table_x, precision=HIGH)
    plane_cells = planes * half_y
    placer = (recv_pos[0].astype(jnp.int32)[None, :] == jnp.arange(plane_cells)[:, None]).astype(
        jnp.float32
    )
    plane_grid = jnp.einsum("cq,vqk->vck", placer, spectral_rows, precision=HIGH)
    plane_grid = plane_grid.reshape(6, planes, half_y, 2 * NX)
    y_spectrum = middle_transform(plane_grid, half_y, NY, NY, -1, "ky,vzyx->vzkx")
    z_spectrum = middle_transform(
        lax.all_to_all(y_spectrum, "slab", split_axis=2, concat_axis=1, tiled=True),
        half_z,
        NZ,
        NZ,
        -1,
        "kz,vzyx->vkyx",
    )
    image = apply_kernel(z_spectrum, green)
    z_back = middle_transform(image, NZ, NZ, half_z, 1, "kz,vzyx->vkyx")
    fields = middle_transform(
        lax.all_to_all(z_back, "slab", split_axis=1, concat_axis=2, tiled=True),
        NY,
        NY,
        half_y,
        1,
        "ky,vzyx->vzkx",
    )
    flat_fields = fields.reshape(6, plane_cells, 2 * NX)
    picked = jnp.einsum("cq,vck->vqk", placer, flat_fields, precision=HIGH)
    table_back = dft_table(NX, NX, row_len, 1)
    back_rows = jnp.einsum("vqk,kx->vqx", picked, table_back, precision=HIGH)
    returned = jnp.einsum(
        "qr,vqx->vrx",
        pack_float,
        lax.all_to_all(back_rows, "slab", split_axis=1, concat_axis=1, tiled=True),
        precision=HIGH,
    )
    row_mask = occupied.astype(jnp.float32)[None, :, None]
    alpha_re = inv_alpha[:, :row_len]
    alpha_im = inv_alpha[:, row_len:]
    dip_re = dipoles[:, :, :row_len]
    dip_im = dipoles[:, :, row_len:]
    out_re = alpha_re * dip_re - alpha_im * dip_im - returned[:, :, :row_len]
    out_im = alpha_re * dip_im + alpha_im * dip_re - returned[:, :, row_len:]
    return jnp.concatenate([out_re, out_im], axis=-1) * row_mask


BF = jnp.bfloat16
F32 = jnp.float32
SYM = ((0, 1, 2), (1, 3, 4), (2, 4, 5))


def split(values):
    high = values.astype(BF)
    return high, (values - high.astype(F32)).astype(BF)


def left3(values):
    high, low = split(values)
    return jnp.concatenate([high, high, low], axis=1)


def right3(values):
    high, low = split(values)
    return jnp.concatenate([high, low, high], axis=0)


def mm(left, right):
    return jnp.dot(left, right, preferred_element_type=F32)


def trig(rows, cols, length):
    angles = 2.0 * np.pi * (np.arange(rows)[:, None] * np.arange(cols)[None, :] % length) / length
    return np.cos(angles), np.sin(angles)


def stack3(table):
    return right3(jnp.asarray(table.astype(np.float32)))


def spectral_kernel(
    rows_ref, green_ref, ty_ref, tz_ref, tx_ref, tb_ref, out_ref,
    xs, ez, ey, spec, img, acc,
):
    step = pl.program_id(0)
    steps = pl.num_programs(0)
    n_dev, comps, per_dev, width = out_ref.shape
    n_rows = n_dev * per_dev
    kz_block, ky_count = green_ref.shape[1], green_ref.shape[2]
    nx = green_ref.shape[3] // 2
    cells = kz_block * ky_count

    @pl.when(step == 0)
    def _():
        acc[...] = jnp.zeros_like(acc)
        sites = rows_ref[:, comps].reshape(n_rows, width)
        first_ky = pl.multiple_of(lax.axis_index("slab") * ky_count, ky_count)
        for axis, (table, dest, first) in enumerate(((ty_ref, ey, first_ky), (tz_ref, ez, 0))):
            half = table.shape[2]
            column = sites[:, axis : axis + 1].astype(jnp.int32)
            hot = (lax.broadcasted_iota(jnp.int32, (n_rows, half), 1) == column).astype(F32)
            for part in range(2):
                dest[part] = lax.dot_general(
                    table[part, pl.ds(first, dest.shape[1])], hot, (((1,), (1,)), ((), ())), precision=HIGH, preferred_element_type=F32
                )
        for c in range(comps):
            rows = rows_ref[:, c].reshape(n_rows, width)
            x = mm(left3(rows), tx_ref[...])
            x_re, x_im = x[:, :nx], x[:, nx:]
            xs[0, c] = right3(x_re)
            xs[1, c] = right3(x_im)
            xs[2, c] = right3(x_re + x_im)

    zc = ez[0, pl.ds(step * kz_block, kz_block), :][:, None, :]
    zs = ez[1, pl.ds(step * kz_block, kz_block), :][:, None, :]
    yc = ey[0][None]
    ys = ey[1][None]
    a = (zc * yc - zs * ys).reshape(cells, n_rows)
    b = -(zc * ys + zs * yc).reshape(cells, n_rows)
    fa, fb, fab = left3(a), left3(b), left3(a + b)
    for c in range(comps):
        p1 = mm(fa, xs[0, c])
        p2 = mm(fb, xs[1, c])
        p3 = mm(fab, xs[2, c])
        spec[c, 0] = p1 - p2
        spec[c, 1] = p3 - p1 - p2

    a_t = a.T
    b_t = -b.T
    ga, gb, gab = left3(a_t), left3(b_t), left3(a_t + b_t)

    kz_chunk = max(1, 16 // ky_count)
    chunk = kz_chunk * ky_count

    def apply_chunk(j):
        row = j * chunk
        for lane in range(0, nx, 128):
            g = [
                [
                    green_ref[m, pl.ds(j * kz_chunk, kz_chunk), :, pl.ds(part * nx + lane, 128)].reshape(chunk, 128)
                    for part in range(2)
                ]
                for m in range(6)
            ]
            for v in range(comps // 3):
                s = [[spec[3 * v + o, part, pl.ds(row, chunk), pl.ds(lane, 128)] for part in range(2)] for o in range(3)]
                for t in range(3):
                    re = im = None
                    for o in range(3):
                        k_re, k_im = g[SYM[t][o]]
                        s_re, s_im = s[o]
                        d_re = k_re * s_re - k_im * s_im
                        d_im = k_re * s_im + k_im * s_re
                        re = d_re if re is None else re + d_re
                        im = d_im if im is None else im + d_im
                    for kind, value in enumerate((re, im, re + im)):
                        high, low = split(value)
                        img[kind, 3 * v + t, 0, pl.ds(row, chunk), pl.ds(lane, 128)] = high
                        img[kind, 3 * v + t, 1, pl.ds(row, chunk), pl.ds(lane, 128)] = low

    for j in range(kz_block // kz_chunk):
        apply_chunk(j)

    for c in range(comps):
        for kind, left in enumerate((ga, gb, gab)):
            high = img[kind, c, 0]
            low = img[kind, c, 1]
            acc[kind, c] += mm(left, jnp.concatenate([high, low, high], axis=0))

    @pl.when(step == steps - 1)
    def _():
        for c in range(comps):
            p1, p2, p3 = acc[0, c], acc[1, c], acc[2, c]
            both = jnp.concatenate([p1 - p2, p3 - p1 - p2], axis=1)
            out_ref[:, c] = mm(left3(both), tb_ref[...]).reshape(n_dev, per_dev, width)


def spectral(rows, green, nx, ny, nz):
    n_dev, planes, per_dev, width = rows.shape
    comps = planes - 1
    n_rows = n_dev * per_dev
    ky_count = green.shape[2]
    row_len = width // 2
    kz_block = 256 // ky_count
    cos_x, sin_x = trig(row_len, nx, nx)
    forward_x = np.block([[cos_x, -sin_x], [sin_x, cos_x]])
    back_x = np.block([[cos_x.T, sin_x.T], [-sin_x.T, cos_x.T]]) / float(nx * ny * nz)
    table_y = jnp.asarray(np.stack(trig(ny, ny // 2, ny)).astype(np.float32))
    table_z = jnp.asarray(np.stack(trig(nz, nz // 2, nz)).astype(np.float32))
    whole = lambda: pl.BlockSpec(memory_space=pltpu.VMEM)
    return pl.pallas_call(
        spectral_kernel,
        grid=(nz // kz_block,),
        out_shape=jax.ShapeDtypeStruct((n_dev, comps, per_dev, width), F32),
        in_specs=[
            whole(),
            pl.BlockSpec((6, kz_block, ky_count, 2 * nx), lambda i: (0, i, 0, 0)),
            whole(),
            whole(),
            whole(),
            whole(),
        ],
        out_specs=pl.BlockSpec(memory_space=pltpu.VMEM),
        scratch_shapes=[
            pltpu.VMEM((3, comps, 3 * n_rows, nx), BF),
            pltpu.VMEM((2, nz, n_rows), F32),
            pltpu.VMEM((2, ky_count, n_rows), F32),
            pltpu.VMEM((comps, 2, kz_block * ky_count, nx), F32),
            pltpu.VMEM((3, comps, 2, kz_block * ky_count, nx), BF),
            pltpu.VMEM((3, comps, n_rows, nx), F32),
        ],
        compiler_params=pltpu.CompilerParams(vmem_limit_bytes=60000 * 1024),
    )(rows, green, table_y, table_z, stack3(forward_x), stack3(back_x))


def place(n_dev):
    me = lax.axis_index("slab")
    return me, me // 4, (me // 2) % 2, me % 2, n_dev // 4


def slot_of(z, x, core):
    return (z * 2 + x) * 2 + core


def greet(peers):
    barrier = pltpu.get_barrier_semaphore()
    for peer in peers:
        pl.semaphore_signal(barrier, inc=1, device_id={"slab": peer}, device_id_type=pl.DeviceIdType.MESH)
    pl.semaphore_wait(barrier, len(peers))


def send(src, dst, send_sem, recv_sem, peer):
    copy = pltpu.make_async_remote_copy(
        src_ref=src,
        dst_ref=dst,
        send_sem=send_sem,
        recv_sem=recv_sem,
        device_id={"slab": peer},
        device_id_type=pl.DeviceIdType.MESH,
    )
    copy.start()
    return copy


def site_columns(site_ref):
    per_dev = site_ref.shape[1]
    row = lax.broadcasted_iota(jnp.int32, (per_dev, per_dev), 0)
    col = lax.broadcasted_iota(jnp.int32, (per_dev, per_dev), 1)
    return [
        jnp.sum(jnp.where(row == col, site_ref[axis : axis + 1, :].astype(F32), 0.0), axis=1, keepdims=True)
        for axis in range(2)
    ]


CHUNKS = 3


class Sender:
    def __init__(self, send_sems, recv_sems):
        self.send_sems, self.recv_sems = send_sems, recv_sems
        self.copies = {}

    def start(self, key, src, dst, peer):
        k = len(self.copies)
        self.copies[key] = send(src, dst, self.send_sems.at[k], self.recv_sems.at[k], peer)

    def arrived(self, key):
        self.copies[key].wait_recv()

    def sent(self):
        for copy in self.copies.values():
            copy.wait_send()


def gather_kernel(dip_ref, site_ref, all_ref, send_z, recv_z, send_x, recv_x, send_c, recv_c):
    n_dev = all_ref.shape[0]
    comps, per_dev, width = dip_ref.shape
    me, z, x, core, depth = place(n_dev)
    all_ref[me, pl.ds(0, comps)] = dip_ref[...]
    y_col, z_col = site_columns(site_ref)
    lane = lax.broadcasted_iota(jnp.int32, (per_dev, width), 1)
    all_ref[me, comps] = jnp.where(lane == 0, y_col, z_col)
    x_peer, c_peer = slot_of(z, 1 - x, core), slot_of(z, x, 1 - core)
    greet([x_peer, c_peer, *(slot_of((z + d) % depth, x, core) for d in range(1, depth))])
    order = sorted(range(1, depth), key=lambda d: min(d, depth - d))
    zs, xs, cs = {}, {}, {}
    for d in order:
        zs[d] = send(all_ref.at[me], all_ref.at[me], send_z.at[d], recv_z.at[d], slot_of((z + d) % depth, x, core))

    def pass_on(d):
        slot = all_ref.at[slot_of((z - d + depth) % depth, x, core)]
        xs[d] = send(slot, slot, send_x.at[d], recv_x.at[d], x_peer)
        cs[d, 0] = send(slot, slot, send_c.at[d], recv_c.at[d], c_peer)

    def cross(d):
        xs[d].wait_recv()
        slot = all_ref.at[slot_of((z - d + depth) % depth, 1 - x, core)]
        cs[d, 1] = send(slot, slot, send_c.at[depth + d], recv_c.at[depth + d], c_peer)

    pass_on(0)
    before = 0
    for d in order:
        zs[d].wait_recv()
        pass_on(d)
        cross(before)
        before = d
    cross(before)
    for copy in cs.values():
        copy.wait_recv()
    for copy in [*zs.values(), *xs.values(), *cs.values()]:
        copy.wait_send()


def gather_rows(dipoles, row_site):
    n_dev = lax.axis_size("slab")
    depth = n_dev // 4
    comps, per_dev, width = dipoles.shape
    dma = pltpu.SemaphoreType.DMA
    return pl.pallas_call(
        gather_kernel,
        out_shape=jax.ShapeDtypeStruct((n_dev, comps + 1, per_dev, width), F32),
        in_specs=[pl.BlockSpec(memory_space=pltpu.VMEM)] * 2,
        out_specs=pl.BlockSpec(memory_space=pltpu.VMEM),
        scratch_shapes=[dma((depth,)), dma((depth,)), dma((depth,)), dma((depth,)), dma((2 * depth,)), dma((2 * depth,))],
        compiler_params=pltpu.CompilerParams(collective_id=0, has_side_effects=True),
    )(dipoles, row_site)


def reduce_kernel(part_ref, dip_ref, alpha_ref, site_ref, out_ref, got_c, got, total, send_sems, recv_sems):
    n_dev, comps, per_dev, width = part_ref.shape
    row_len = width // 2
    me, z, x, core, depth = place(n_dev)
    half = depth // 2
    at_z = lambda d, col: slot_of((z + d + depth) % depth, col, core)
    x_peer, c_peer = slot_of(z, 1 - x, core), slot_of(z, x, 1 - core)
    greet([x_peer, c_peer, at_z(1, x), at_z(-1, x)])
    way = 1 - 2 * core
    net = Sender(send_sems, recv_sems)
    span = comps // CHUNKS
    col_of = lambda col: x if col == 0 else 1 - x
    offsets = [d for k in range(half - 1, 0, -1) for d in (k, -k)]
    order = [(half, 1), *((d, 1) for d in offsets), (half, 0), *((d, 0) for d in offsets), (0, 1), (0, 0)]
    got_at = {}

    def piece(ref, q):
        return ref.at[pl.ds(q * span, span)]

    def move(kind, q, d, col, peer):
        at = got_at.setdefault((kind, d, col), len(got_at))
        net.start((kind, q, d, col), piece(total.at[order.index((d, col))], q), piece(got.at[at], q), peer)

    def add(q, d, col, *keys):
        chunk = pl.ds(q * span, span)
        value = total[order.index((d, col)), chunk]
        for kind, from_d, from_col in keys:
            net.arrived((kind, q, from_d, from_col))
            value = value + got[got_at[kind, from_d, from_col], chunk]
        total[order.index((d, col)), chunk] = value

    for q in range(CHUNKS):
        for k, (d, col) in enumerate(order):
            slot = slot_of((z + d + depth) % depth, col_of(col), 1 - core)
            net.start(("c", q, d, col), piece(part_ref.at[slot], q), piece(got_c.at[k], q), c_peer)

    def both_cores(q, d, col):
        net.arrived(("c", q, d, col))
        k = order.index((d, col))
        chunk = pl.ds(q * span, span)
        total[k, chunk] = part_ref[at_z(d, col_of(col)), chunk] + got_c[k, chunk]

    for q in range(CHUNKS):
        both_cores(q, half, 1)
        move("x", q, half, 1, x_peer)
        for d in offsets:
            both_cores(q, d, 1)
            if abs(d) == half - 1:
                move("z", q, d, 1, at_z(1 if d > 0 else -1, x))
    for k in range(half - 2, 0, -1):
        for q in range(CHUNKS):
            for d in (k, -k):
                add(q, d, 1, ("z", d + (1 if d > 0 else -1), 1))
                move("z", q, d, 1, at_z(1 if d > 0 else -1, x))
    for q in range(CHUNKS):
        both_cores(q, half, 0)
        add(q, half, 0, ("x", half, 1))
        at = got_at.setdefault("h", len(got_at))
        net.start(("h", q), piece(total.at[order.index((half, 0))], q), piece(got.at[at], q), at_z(way, x))
        for d in (0, *offsets):
            both_cores(q, d, 1 if d == 0 else 0)
        add(q, 0, 1, ("z", 1, 1), ("z", -1, 1))
        move("x", q, 0, 1, x_peer)
    for k in range(half - 1, 0, -1):
        for q in range(CHUNKS):
            for d in (k, -k):
                s = 1 if d > 0 else -1
                if k == half - 1:
                    if d > 0:
                        net.arrived(("h", q))
                    chunk = pl.ds(q * span, span)
                    index = order.index((d, 0))
                    extra = jnp.where(way == s, got[got_at["h"], chunk], 0.0)
                    total[index, chunk] = total[index, chunk] + extra
                else:
                    add(q, d, 0, ("z", d + s, 0))
                move("z", q, d, 0, at_z(s, x))
    a_re, a_im = alpha_ref[:, :row_len], alpha_ref[:, row_len:]
    y_col, _ = site_columns(site_ref)
    live = y_col >= 0.0
    own = order.index((0, 0))
    for q in range(CHUNKS):
        both_cores(q, 0, 0)
        add(q, 0, 0, ("x", 0, 1), ("z", 1, 0), ("z", -1, 0))
        for c in range(q * span, (q + 1) * span):
            v_re, v_im = total[own, c, :, :row_len], total[own, c, :, row_len:]
            d_re, d_im = dip_ref[c, :, :row_len], dip_ref[c, :, row_len:]
            o_re = a_re * d_re - a_im * d_im - v_re
            o_im = a_re * d_im + a_im * d_re - v_im
            out_ref[c] = jnp.where(live, jnp.concatenate([o_re, o_im], axis=1), 0.0)
    net.sent()


def reduce_rows(partial, dipoles, inv_alpha, row_site):
    n_dev, *block = partial.shape
    count = CHUNKS * 2 * n_dev
    hold = lambda slots: pltpu.VMEM((slots, *block), F32)
    return pl.pallas_call(
        reduce_kernel,
        out_shape=jax.ShapeDtypeStruct(dipoles.shape, F32),
        in_specs=[pl.BlockSpec(memory_space=pltpu.VMEM)] * 4,
        out_specs=pl.BlockSpec(memory_space=pltpu.VMEM),
        scratch_shapes=[
            hold(n_dev // 2), hold(n_dev // 2), hold(n_dev // 2),
            pltpu.SemaphoreType.DMA((count,)), pltpu.SemaphoreType.DMA((count,)),
        ],
        compiler_params=pltpu.CompilerParams(collective_id=1, has_side_effects=True),
    )(partial, dipoles, inv_alpha, row_site)


def rows_body(dipoles, inv_alpha, row_site, green):
    nz = green.shape[1]
    nx = green.shape[3] // 2
    ny = green.shape[2] * lax.axis_size("slab")
    rows = gather_rows(dipoles, row_site)
    partial = spectral(rows, green, nx, ny, nz)
    return reduce_rows(partial, dipoles, inv_alpha, row_site)


def body(dipoles, inv_alpha, row_site, green):
    n_rows = dipoles.shape[1] * lax.axis_size("slab")
    spectra_bytes = 4 * dipoles.shape[0] * n_rows * green.shape[3]
    if spectra_bytes <= 4 * 2**20 and green.shape[2] % 8 == 0 and lax.axis_size("slab") % 16 == 0:
        return rows_body(dipoles, inv_alpha, row_site, green)
    return planes_body(dipoles, inv_alpha, row_site, green)


def solution(mesh):
    return jax.shard_map(
        body,
        mesh=mesh,
        in_specs=(
            P("rep", "slab", None),
            P("slab", None),
            P(None, "slab"),
            P(None, None, "slab", None),
        ),
        out_specs=P("rep", "slab", None),
        check_vma=False,
    )
```
